32 devices in a mesh: fsdp: 4 (over z), tp: 8 (over y, x, core).
Axes of the slice: x: 2, y: 2, z: 4, core: 2. Of those that a mesh axis runs over, the one named last changes fastest.
Arguments:
- tokens: bfloat16 [8192, 2048], P(('fsdp', 'tp')), may hold values from -6 to 6
- seq_len: int32 [8], replicated, may hold values from 256 to 1792, as said below
- seq_group: int32 [8], replicated, may hold values from 0 to 3, as said below
- ln1_gain: float32 [2048], replicated, may hold values from 0.1 to 1.9
- ln1_bias: float32 [2048], replicated, may hold values from -1.75 to 1.75
- qkv_weight: bfloat16 [2048, 3, 2048], P('fsdp', None, 'tp'), may hold values from -0.125 to 0.125
- qv_bias: float32 [2, 2048], P(None, 'tp'), may hold values from -0.625 to 0.625
- out_weight: bfloat16 [2048, 2048], P('tp', 'fsdp'), may hold values from -0.75 to 0.75
- out_bias: float32 [2048], replicated, may hold values from -1.75 to 1.75
- ln2_gain: float32 [2048], replicated, may hold values from 0.1 to 1.9
- ln2_bias: float32 [2048], replicated, may hold values from -1.75 to 1.75
- up_weight: bfloat16 [2048, 8192], P('fsdp', 'tp'), may hold values from -0.125 to 0.125
- up_bias: float32 [8192], P('tp'), may hold values from -1.75 to 1.75
- down_weight: bfloat16 [8192, 2048], P('tp', 'fsdp'), may hold values from -0.0625 to 0.0625
- down_bias: float32 [2048], replicated, may hold values from -1.75 to 1.75
- out_grad: bfloat16 [8192, 2048], P(('fsdp', 'tp')), may hold values from -6 to 6
Outputs:
- layer_out: bfloat16 [8192, 2048], P(('fsdp', 'tp'))
- tokens_grad: bfloat16 [8192, 2048], P(('fsdp', 'tp'))
- grad_ln1_gain: float32 [2048], replicated
- grad_ln1_bias: float32 [2048], replicated
- grad_qkv_weight: float32 [2048, 3, 2048], P('fsdp', None, 'tp')
- grad_qv_bias: float32 [2, 2048], P(None, 'tp')
- grad_out_weight: float32 [2048, 2048], P('tp', 'fsdp')
- grad_out_bias: float32 [2048], replicated
- grad_ln2_gain: float32 [2048], replicated
- grad_ln2_bias: float32 [2048], replicated
- grad_up_weight: float32 [2048, 8192], P('fsdp', 'tp')
- grad_up_bias: float32 [8192], P('tp')
- grad_down_weight: float32 [8192, 2048], P('tp', 'fsdp')
- grad_down_bias: float32 [2048], replicated
The draws below stay inside these ranges and needn't reach their ends.
Inputs may be any that keep to these rules, and one draw needn't show every extreme that they name: `seq_group`: every group holds exactly two sequences. `seq_len`: every length is a multiple of 256; the two sequences of a group take at most 2048 rows together, and in every draw some group is filled exactly.
All inputs are finite; a program needn't handle non-finite values.
Results may differ from the reference program's by a relative error of at most 0.02.
Values may be sent and summed in bfloat16 or wider, within the bound.
No kernel may reach another device: no remote copies, remote signals or barrier semaphores. Data moves between devices by JAX's collectives and lax.ppermute only.
A program may use at most 192 MiB of HBM per device.

```python
import jax
import jax.numpy as jnp
from jax import lax

D = 2048
HEADS = 16
HEAD_DIM = 128
FF = 8192
TOK_DEV = 2048
TOKENS = 8192
SEQS = 8
UNIT = 256
N_FSDP = 4


def sequence_layout(key):
    base = jax.random.fold_in(key, 7)
    seq_order = jax.random.permutation(jax.random.fold_in(base, 1), SEQS)
    group_count = SEQS // 2
    first_units = jax.random.randint(jax.random.fold_in(base, 2), (group_count,), 2, 8)
    second_units = jax.random.randint(jax.random.fold_in(base, 3), (group_count,), 1, 9 - first_units)
    full_group = jax.random.randint(jax.random.fold_in(base, 4), (), 0, group_count)
    is_full = jnp.arange(group_count) == full_group
    first_units = jnp.where(is_full, 7, first_units)
    second_units = jnp.where(is_full, 1, second_units)
    group_of = seq_order // 2
    slot_of = seq_order % 2
    units = jnp.where(slot_of == 0, first_units[group_of], second_units[group_of])
    return (group_of.astype(jnp.int32), (units * UNIT).astype(jnp.int32))


def draw_seq_group(key, part):
    return sequence_layout(key)[0]


def draw_seq_len(key, part):
    return sequence_layout(key)[1]


def levels(own_key, extent, shards, least, top_value):
    level, own = 1.0, jax.random.fold_in(own_key, 6)
    for axis_at, blocks in shards:
        steps = jnp.exp(jax.random.uniform(jax.random.fold_in(own, axis_at), (blocks,), jnp.float32, least / len(shards), top_value / len(shards)))
        level = level * jnp.repeat(steps, extent[axis_at] // blocks).reshape([-1 if axis == axis_at else 1 for axis in range(len(extent))])
    return level


def gaussian(stream_key, shape, scale, most, split=(), held_as=jnp.bfloat16):
    level = levels(stream_key, shape, split, -0.22, 0.18) if split else 1.0
    array = jax.random.normal(stream_key, shape, jnp.float32) * scale * level
    return jnp.minimum(jnp.maximum(array, -most), most).astype(held_as)


def setup_inputs(seed: int = 0) -> dict:
    keys = jax.random.split(jax.random.key(seed), 17)
    tokens = gaussian(keys[0], (TOKENS, D), 1.0, 6.0, ((0, 32),))
    seq_len = draw_seq_len(jax.random.fold_in(keys[16], 71), 0)
    seq_group = draw_seq_group(jax.random.fold_in(keys[16], 71), 0)
    ln1_gain = jnp.clip(1.0 + 0.18 * jax.random.normal(keys[3], (D,), jnp.float32), 0.1, 1.9)
    ln1_bias = gaussian(keys[4], (D,), 0.3, 1.75, (), jnp.float32)
    qkv_weight = gaussian(keys[5], (D, 3, D), D ** -0.5, 0.125, ((0, 4), (2, 8)))
    qv_bias = gaussian(keys[6], (2, D), 0.1, 0.625, ((1, 8),), jnp.float32)
    out_weight = gaussian(keys[7], (D, D), 64 ** -0.5, 0.75, ((0, 8), (1, 4)))
    out_bias = gaussian(keys[8], (D,), 0.3, 1.75, (), jnp.float32)
    ln2_gain = jnp.clip(1.0 + 0.18 * jax.random.normal(keys[9], (D,), jnp.float32), 0.1, 1.9)
    ln2_bias = gaussian(keys[10], (D,), 0.3, 1.75, (), jnp.float32)
    up_weight = gaussian(keys[11], (D, FF), D ** -0.5, 0.125, ((0, 4), (1, 8)))
    up_bias = gaussian(keys[12], (FF,), 0.3, 1.75, ((0, 8),), jnp.float32)
    down_weight = gaussian(keys[13], (FF, D), FF ** -0.5, 0.0625, ((0, 8), (1, 4)))
    down_bias = gaussian(keys[14], (D,), 0.3, 1.75, (), jnp.float32)
    out_grad = gaussian(keys[15], (TOKENS, D), 1.0, 6.0, ((0, 32),))
    return {"tokens": tokens, "seq_len": seq_len, "seq_group": seq_group, "ln1_gain": ln1_gain, "ln1_bias": ln1_bias, "qkv_weight": qkv_weight, "qv_bias": qv_bias, "out_weight": out_weight, "out_bias": out_bias, "ln2_gain": ln2_gain, "ln2_bias": ln2_bias, "up_weight": up_weight, "up_bias": up_bias, "down_weight": down_weight, "down_bias": down_bias, "out_grad": out_grad}


EPSILON = 1e-05
MASKED = -1e+30

@jax.custom_vjp
def low(v):
    return lax.optimization_barrier(v.astype(jnp.bfloat16)).astype(jnp.float32)

@jax.custom_vjp
def low_back(v):
    return v

def low_keep(v):
    return (low(v), None)

def low_pass(kept, grad):
    return (grad,)

def back_keep(v):
    return (v, None)

def back_low(kept, grad):
    return (low(grad),)
low.defvjp(low_keep, low_pass)
low_back.defvjp(back_keep, back_low)

def layer_norm(values, gain_vec, bias_vec):
    row_mean = lax.optimization_barrier(jnp.mean(values, axis=-1, keepdims=True))
    centred = values - row_mean
    variance = lax.optimization_barrier(jnp.mean(centred * centred, axis=-1, keepdims=True))
    return centred * lax.rsqrt(variance + EPSILON) * gain_vec + bias_vec

def gelu_tanh(values):
    return jax.nn.gelu(values, approximate=True)

def row_keys(seq_len, seq_group, group_id, row_count):
    seq_count = seq_len.shape[0]
    seq_order = jnp.arange(seq_count, dtype=jnp.int32)
    same_before = (seq_group[None, :] == seq_group[:, None]) & (seq_order[None, :] < seq_order[:, None])
    starts = lax.optimization_barrier(jnp.sum(jnp.where(same_before, seq_len[None, :], 0), axis=1)).astype(jnp.int32)
    places = jnp.arange(row_count, dtype=jnp.int32)[:, None]
    inside = (seq_group[None, :] == group_id) & (starts[None, :] <= places) & (places < starts[None, :] + seq_len[None, :])
    holder = lax.optimization_barrier(jnp.sum(jnp.where(inside, seq_order[None, :] + 1, 0), axis=1)).astype(jnp.int32)
    return jnp.where(holder > 0, holder - 1, seq_count + places[:, 0]).astype(jnp.int32)

def attend_group(operands):
    qkv_group, group_keys = operands
    queries = qkv_group[:, 0]
    keys_mat = qkv_group[:, 1]
    values = qkv_group[:, 2]
    scores = jnp.einsum('qhd,khd->hqk', queries, keys_mat, precision=lax.Precision.HIGHEST) * HEAD_DIM ** (-0.5)
    scores = low_back(scores)
    positions = jnp.arange(group_keys.shape[0], dtype=jnp.int32)
    allowed = (group_keys[:, None] == group_keys[None, :]) & (positions[None, :] <= positions[:, None])
    scores = jnp.where(allowed[None], scores, MASKED)
    probs = jax.nn.softmax(scores, axis=-1)
    context = jnp.einsum('hqk,khd->qhd', low(probs), values, precision=lax.Precision.HIGHEST)
    return context.reshape(group_keys.shape[0], HEADS * HEAD_DIM)

def reference(tokens, seq_len, seq_group, ln1_gain, ln1_bias, qkv_weight, qv_bias, out_weight, out_bias, ln2_gain, ln2_bias, up_weight, up_bias, down_weight, down_bias, out_grad):

    def keys_of(group_id):
        return row_keys(seq_len, seq_group, group_id, TOK_DEV)
    all_keys = jax.vmap(keys_of)(jnp.arange(N_FSDP, dtype=jnp.int32))

    def forward(inputs, gain_one, bias_one, qkv_mat, qv_shift, out_mat, out_shift, gain_two, bias_two, up_mat, up_shift, down_mat, down_shift):
        norm1 = low(layer_norm(inputs, gain_one, bias_one))
        shift_full = jnp.stack([qv_shift[0], jnp.zeros_like(qv_shift[0]), qv_shift[1]])
        qkv = jnp.einsum('td,dcn->tcn', norm1, qkv_mat, precision=lax.Precision.HIGHEST) + shift_full[None]
        qkv = low_back(low(qkv))
        groups_qkv = qkv.reshape(N_FSDP, TOK_DEV, 3, HEADS, HEAD_DIM)
        context = lax.map(jax.checkpoint(attend_group), (groups_qkv, all_keys))
        context = low_back(low(context.reshape(TOKENS, D)))
        projected = low_back(jnp.dot(context, out_mat, precision=lax.Precision.HIGHEST))
        middle = inputs + projected + out_shift
        norm2 = low(layer_norm(middle, gain_two, bias_two))
        pre = low_back(jnp.dot(norm2, up_mat, precision=lax.Precision.HIGHEST) + up_shift)
        act = low(gelu_tanh(pre))
        branch = low_back(jnp.dot(act, down_mat, precision=lax.Precision.HIGHEST))
        return middle + branch + down_shift
    floats = [arg.astype(jnp.float32) for arg in (tokens, ln1_gain, ln1_bias, qkv_weight, qv_bias, out_weight, out_bias, ln2_gain, ln2_bias, up_weight, up_bias, down_weight, down_bias)]
    result, pull_back = jax.vjp(forward, *floats)
    gradients = pull_back(out_grad.astype(jnp.float32))
    return (result.astype(jnp.bfloat16), gradients[0].astype(jnp.bfloat16), gradients[1], gradients[2], gradients[3], gradients[4], gradients[5], gradients[6], gradients[7], gradients[8], gradients[9], gradients[10], gradients[11], gradients[12])
```

```python
import jax
import jax.numpy as jnp
from jax import lax
from jax.sharding import PartitionSpec as P

HEAD_DIM = 128


EPSILON = 1e-05
MASKED = -1e30


def layer_norm(values, gain_vec, bias_vec):
    row_mean = jnp.mean(values, axis=-1, keepdims=True)
    centred = values - row_mean
    variance = jnp.mean(centred * centred, axis=-1, keepdims=True)
    return centred * lax.rsqrt(variance + EPSILON) * gain_vec + bias_vec


def gelu_tanh(values):
    return jax.nn.gelu(values, approximate=True)


def row_keys(seq_len, seq_group, group_id, row_count):
    seq_count = seq_len.shape[0]
    seq_order = jnp.arange(seq_count, dtype=jnp.int32)
    same_before = (seq_group[None, :] == seq_group[:, None]) & (
        seq_order[None, :] < seq_order[:, None]
    )
    starts = jnp.sum(jnp.where(same_before, seq_len[None, :], 0), axis=1)
    places = jnp.arange(row_count, dtype=jnp.int32)[:, None]
    inside = (
        (seq_group[None, :] == group_id)
        & (starts[None, :] <= places)
        & (places < starts[None, :] + seq_len[None, :])
    )
    holder = jnp.sum(jnp.where(inside, seq_order[None, :] + 1, 0), axis=1)
    return jnp.where(holder > 0, holder - 1, seq_count + places[:, 0])


def contract_rows(left, right):
    return lax.dot_general(
        left, right, (((0,), (0,)), ((), ())), preferred_element_type=jnp.float32
    )


def contract_cols(left, right):
    return lax.dot_general(
        left, right, (((1,), (1,)), ((), ())), preferred_element_type=jnp.float32
    )


SWAP_TP = 8


def exchange(piece, mask):
    return lax.ppermute(piece, "tp", [(at, at ^ mask) for at in range(SWAP_TP)])


def gather_rows(piece):
    if lax.axis_size("tp") != SWAP_TP:
        return lax.all_gather(piece, "tp", axis=0, tiled=True)
    half = piece.shape[0] // 2
    from_x = exchange(piece, 2)
    from_y = exchange(piece, 4)
    own_twin = exchange(piece, 1)
    far_low = exchange(from_x[:half], 4)
    far_high = exchange(from_y[half:], 2)
    parts = [from_x, from_y, far_low, far_high]
    twins = [exchange(part, 1) for part in parts]
    return jnp.concatenate([piece, *parts, own_twin, *twins], axis=0)


def add_low(left, right):
    return (left.astype(jnp.float32) + right.astype(jnp.float32)).astype(jnp.bfloat16)


def scatter_rows(product):
    tp_count = lax.axis_size("tp")
    if tp_count != SWAP_TP:
        return lax.psum_scatter(product(0, None), "tp", scatter_dimension=0, tiled=True).astype(
            jnp.float32
        )
    twin_part = product(1, 2)
    own_part = product(0, 2)
    rows = own_part.shape[0] // 4
    half = rows // 2
    both = add_low(own_part, exchange(twin_part, 1))
    home, to_x, to_y, far = (both[at * rows : (at + 1) * rows] for at in range(4))
    far_low = exchange(far[:half], 2)
    far_high = exchange(far[half:], 4)
    x_low = exchange(to_x[:half], 2)
    y_high = exchange(to_y[half:], 4)
    x_high = exchange(add_low(to_x[half:], far_high), 2)
    y_low = exchange(add_low(to_y[:half], far_low), 4)
    wide = [part.astype(jnp.float32) for part in (x_low, x_high, y_low, y_high)]
    return (
        home.astype(jnp.float32)
        + jnp.concatenate(wide[:2], axis=0)
        + jnp.concatenate(wide[2:], axis=0)
    )


def sum_over(vector, axis):
    count = lax.axis_size(axis)
    terms = [vector] + [
        lax.ppermute(vector, axis, [(at, at ^ step) for at in range(count)])
        for step in range(1, count)
    ]
    while len(terms) > 1:
        terms = [terms[at] + terms[at + 1] for at in range(0, len(terms), 2)]
    return terms[0]


def block_places(tp_count, tp_index):
    block_at = jnp.arange(tp_count, dtype=jnp.int32)
    if tp_count != SWAP_TP:
        return block_at
    apart = block_at ^ tp_index
    return (apart >> 1) + 4 * (apart & 1)


def take_blocks(rows, places, block_rows):
    return jnp.concatenate(
        [
            lax.dynamic_slice_in_dim(rows, places[at] * block_rows, block_rows, 0)
            for at in range(places.shape[0])
        ],
        axis=0,
    )


def local(
    tokens,
    seq_len,
    seq_group,
    ln1_gain,
    ln1_bias,
    qkv_weight,
    qv_bias,
    out_weight,
    out_bias,
    ln2_gain,
    ln2_bias,
    up_weight,
    up_bias,
    down_weight,
    down_bias,
    out_grad,
):
    tp_count = lax.axis_size("tp")
    tp_index = lax.axis_index("tp")
    own_rows = tokens.shape[0]
    all_rows = own_rows * tp_count
    width = tokens.shape[1]
    head_cols = qkv_weight.shape[2]
    local_heads = head_cols // HEAD_DIM
    ff_cols = up_weight.shape[1]
    scaling = HEAD_DIM ** (-0.5)
    blk_rows = min(512, all_rows)
    blk_count = all_rows // blk_rows
    group_keys = row_keys(seq_len, seq_group, lax.axis_index("fsdp"), all_rows)
    positions = jnp.arange(all_rows, dtype=jnp.int32)
    places = block_places(tp_count, tp_index)
    slot_at = jnp.arange(tp_count, dtype=jnp.int32)
    holders = (2 * (slot_at % 4) + slot_at // 4) ^ tp_index if tp_count == SWAP_TP else slot_at

    def rows_of(rows, first, parts):
        if parts is None:
            return rows
        count = rows.shape[0] // parts
        return rows[first * count : (first + 1) * count]

    def gather_weights():
        return (
            lax.all_gather(qkv_weight, "fsdp", axis=0, tiled=True),
            lax.all_gather(out_weight, "fsdp", axis=1, tiled=True),
            lax.all_gather(up_weight, "fsdp", axis=0, tiled=True),
            lax.all_gather(down_weight, "fsdp", axis=1, tiled=True),
        )

    def block_scores(first_row, queries, keys_mat):
        q_block = lax.dynamic_slice_in_dim(queries, first_row, blk_rows, 0)
        query_keys = lax.dynamic_slice_in_dim(group_keys, first_row, blk_rows, 0)
        query_pos = lax.dynamic_slice_in_dim(positions, first_row, blk_rows, 0)
        allowed = (query_keys[:, None] == group_keys[None, :]) & (
            positions[None, :] <= query_pos[:, None]
        )
        scores = (
            jnp.einsum("qhd,khd->hqk", q_block, keys_mat, preferred_element_type=jnp.float32)
            * scaling
        )
        return (jnp.where(allowed[None], scores, MASKED), q_block)

    inputs = tokens.astype(jnp.float32)
    norm1 = layer_norm(inputs, ln1_gain, ln1_bias).astype(jnp.bfloat16)
    qkv_full, out_full, up_full, down_full = gather_weights()
    qkv_flat = qkv_full.reshape(width, 3 * head_cols)
    qkv_shift = jnp.concatenate([qv_bias[0], jnp.zeros_like(qv_bias[0]), qv_bias[1]])
    norm1_rows = gather_rows(norm1)
    qkv_rows = (
        jnp.dot(
            norm1_rows,
            qkv_flat,
            preferred_element_type=jnp.float32,
        )
        + qkv_shift
    ).astype(jnp.bfloat16)
    qkv_rows = take_blocks(qkv_rows, places, own_rows)
    queries = qkv_rows[:, :head_cols].reshape(all_rows, local_heads, HEAD_DIM)
    keys_mat = qkv_rows[:, head_cols : 2 * head_cols].reshape(all_rows, local_heads, HEAD_DIM)
    values = qkv_rows[:, 2 * head_cols :].reshape(all_rows, local_heads, HEAD_DIM)

    def attend_block(block_id):
        scores, q_block = block_scores(block_id * blk_rows, queries, keys_mat)
        top_score = jnp.max(scores, axis=-1, keepdims=True)
        weights = jnp.exp(scores - top_score)
        weight_sum = jnp.sum(weights, axis=-1, keepdims=True)
        probs = weights / weight_sum
        context_blk = jnp.einsum(
            "hqk,khd->qhd", probs.astype(jnp.bfloat16), values, preferred_element_type=jnp.float32
        )
        return (
            context_blk.astype(jnp.bfloat16).reshape(blk_rows, head_cols),
            (top_score + jnp.log(weight_sum))[..., 0],
        )

    ctx_blocks, lse_blocks = lax.map(attend_block, jnp.arange(blk_count))
    context = take_blocks(ctx_blocks.reshape(all_rows, head_cols), holders, own_rows)
    attn_rows = scatter_rows(
        lambda first, parts: jnp.dot(
            rows_of(context, first, parts), out_full, preferred_element_type=jnp.float32
        ).astype(jnp.bfloat16)
    )
    middle = inputs + attn_rows + out_bias
    norm2 = layer_norm(middle, ln2_gain, ln2_bias).astype(jnp.bfloat16)
    norm_piece = gather_rows(norm2)
    pre = (
        jnp.dot(
            norm_piece,
            up_full,
            preferred_element_type=jnp.float32,
        )
        + up_bias
    )
    act_rows = gelu_tanh(pre).astype(jnp.bfloat16)
    mlp_rows = scatter_rows(
        lambda first, parts: jnp.dot(
            rows_of(act_rows, first, parts), down_full, preferred_element_type=jnp.float32
        ).astype(jnp.bfloat16)
    )
    layer_out = (middle + mlp_rows + down_bias).astype(jnp.bfloat16)
    grad_rows = out_grad.astype(jnp.float32)
    grad_piece = gather_rows(out_grad)
    act_value, gelu_back = jax.vjp(gelu_tanh, pre)
    act_piece = act_value.astype(jnp.bfloat16)
    down_acc = contract_rows(act_piece, grad_piece)
    act_grad = contract_cols(grad_piece, down_full)
    pre_grad = gelu_back(act_grad)[0].astype(jnp.bfloat16)
    up_acc = contract_rows(norm_piece, pre_grad)
    shift_acc = jnp.sum(pre_grad.astype(jnp.float32), axis=0)
    norm2_grad = scatter_rows(
        lambda first, parts: contract_cols(rows_of(pre_grad, first, parts), up_full).astype(
            jnp.bfloat16
        )
    )
    unused_two, ln2_back = jax.vjp(layer_norm, middle, ln2_gain, ln2_bias)
    middle_ln, grad_g2, grad_b2 = ln2_back(norm2_grad)
    middle_grad = grad_rows + middle_ln
    proj_grad = middle_grad.astype(jnp.bfloat16)
    portion = gather_rows(proj_grad)
    out_acc = contract_rows(context, portion)
    ctx_grad_rows = contract_cols(portion, out_full).astype(jnp.bfloat16)
    ctx_grads = take_blocks(ctx_grad_rows, places, own_rows)
    grad_out_w, ctx_grads = (out_acc, ctx_grads)
    ctx_grad = ctx_grads.reshape(all_rows, local_heads, HEAD_DIM)

    def attend_back(carried, block_id):
        key_acc, value_acc = carried
        first_row = block_id * blk_rows
        scores, q_block = block_scores(first_row, queries, keys_mat)
        probs = jnp.exp(scores - lse_blocks[block_id][:, :, None])
        grad_block = lax.dynamic_slice_in_dim(ctx_grad, first_row, blk_rows, 0)
        value_acc = value_acc + jnp.einsum(
            "hqk,qhd->khd",
            probs.astype(jnp.bfloat16),
            grad_block,
            preferred_element_type=jnp.float32,
        )
        prob_grad = jnp.einsum(
            "qhd,khd->hqk", grad_block, values, preferred_element_type=jnp.float32
        )
        row_dot = jnp.sum(probs * prob_grad, axis=-1, keepdims=True)
        score_grad = (probs * (prob_grad - row_dot)).astype(jnp.bfloat16)
        query_grad = (
            jnp.einsum("hqk,khd->qhd", score_grad, keys_mat, preferred_element_type=jnp.float32)
            * scaling
        )
        key_acc = (
            key_acc
            + jnp.einsum("hqk,qhd->khd", score_grad, q_block, preferred_element_type=jnp.float32)
            * scaling
        )
        return ((key_acc, value_acc), query_grad.astype(jnp.bfloat16).reshape(blk_rows, head_cols))

    acc_start = (
        jnp.zeros((all_rows, local_heads, HEAD_DIM), jnp.float32),
        jnp.zeros((all_rows, local_heads, HEAD_DIM), jnp.float32),
    )
    (key_acc, value_acc), query_grads = lax.scan(attend_back, acc_start, jnp.arange(blk_count))
    query_part = query_grads.reshape(all_rows, head_cols)
    value_part = value_acc.reshape(all_rows, head_cols).astype(jnp.bfloat16)
    qkv_grad = jnp.concatenate(
        [query_part, key_acc.reshape(all_rows, head_cols).astype(jnp.bfloat16), value_part], axis=1
    )
    qkv_grad = take_blocks(qkv_grad, holders, own_rows)
    qv_sums = jnp.stack(
        [
            jnp.sum(query_part.astype(jnp.float32), axis=0),
            jnp.sum(value_part.astype(jnp.float32), axis=0),
        ]
    )
    norm1_grad = scatter_rows(
        lambda first, parts: contract_cols(rows_of(qkv_grad, first, parts), qkv_flat).astype(
            jnp.bfloat16
        )
    )
    unused_one, ln1_back = jax.vjp(layer_norm, inputs, ln1_gain, ln1_bias)
    input_ln, grad_g1, grad_b1 = ln1_back(norm1_grad)
    tokens_grad = (middle_grad + input_ln).astype(jnp.bfloat16)
    grad_qkv_flat = contract_rows(norm1_rows, qkv_grad)
    grad_qkv_w = grad_qkv_flat.reshape(width, 3, head_cols)
    shard_qkv, shard_out, shard_up, shard_down = (
        lax.psum_scatter(
            grad_qkv_w.astype(jnp.bfloat16), "fsdp", scatter_dimension=0, tiled=True
        ).astype(jnp.float32),
        lax.psum_scatter(
            grad_out_w.astype(jnp.bfloat16), "fsdp", scatter_dimension=1, tiled=True
        ).astype(jnp.float32),
        lax.psum_scatter(
            up_acc.astype(jnp.bfloat16), "fsdp", scatter_dimension=0, tiled=True
        ).astype(jnp.float32),
        lax.psum_scatter(
            down_acc.astype(jnp.bfloat16), "fsdp", scatter_dimension=1, tiled=True
        ).astype(jnp.float32),
    )
    own_sums = sum_over(jnp.concatenate([qv_sums.reshape(-1), shift_acc]), "fsdp")
    grad_qv = own_sums[: 2 * head_cols].reshape(2, head_cols)
    grad_upb_own = own_sums[2 * head_cols :]
    early = sum_over(
        sum_over(
            jnp.stack([jnp.sum(middle_grad, axis=0), grad_g2, grad_b2, jnp.sum(grad_rows, axis=0)]),
            "fsdp",
        ),
        "tp",
    )
    late = sum_over(sum_over(jnp.stack([grad_g1, grad_b1]), "fsdp"), "tp")
    return (
        layer_out,
        tokens_grad,
        late[0],
        late[1],
        shard_qkv,
        grad_qv,
        shard_out,
        early[0],
        early[1],
        early[2],
        shard_up,
        grad_upb_own,
        shard_down,
        early[3],
    )


def solution(mesh):
    placed = (
        P(("fsdp", "tp"), None),
        P(),
        P(),
        P(),
        P(),
        P("fsdp", None, "tp"),
        P(None, "tp"),
        P("tp", "fsdp"),
        P(),
        P(),
        P(),
        P("fsdp", "tp"),
        P("tp"),
        P("tp", "fsdp"),
        P(),
        P(("fsdp", "tp"), None),
    )
    return jax.shard_map(
        local,
        mesh=mesh,
        in_specs=placed,
        out_specs=(
            P(("fsdp", "tp"), None),
            P(("fsdp", "tp"), None),
            P(),
            P(),
            P("fsdp", None, "tp"),
            P(None, "tp"),
            P("tp", "fsdp"),
            P(),
            P(),
            P(),
            P("fsdp", "tp"),
            P("tp"),
            P("tp", "fsdp"),
            P(),
        ),
        check_vma=False,
    )
```

```python
import jax
import jax.numpy as jnp
from jax import lax
from jax.experimental import pallas as pl
from jax.experimental.pallas import tpu as pltpu
from jax.sharding import PartitionSpec as P

HEAD_DIM = 128


EPSILON = 1e-05
MASKED = -1e30


def layer_norm(values, gain_vec, bias_vec):
    row_mean = jnp.mean(values, axis=-1, keepdims=True)
    centred = values - row_mean
    variance = jnp.mean(centred * centred, axis=-1, keepdims=True)
    return centred * lax.rsqrt(variance + EPSILON) * gain_vec + bias_vec


def gelu_tanh(values):
    return jax.nn.gelu(values, approximate=True)


def contract_rows(left, right):
    return lax.dot_general(
        left, right, (((0,), (0,)), ((), ())), preferred_element_type=jnp.float32
    )


def contract_cols(left, right):
    return lax.dot_general(
        left, right, (((1,), (1,)), ((), ())), preferred_element_type=jnp.float32
    )


SWAP_TP = 8
BLOCK = 256
LOG2_E = 1.4426950408889634


def exchange(piece, mask):
    return lax.ppermute(piece, "tp", [(at, at ^ mask) for at in range(SWAP_TP)])


def gather_rows(piece):
    if lax.axis_size("tp") != SWAP_TP:
        return lax.all_gather(piece, "tp", axis=0, tiled=True)
    half = piece.shape[0] // 2
    from_x = exchange(piece, 2)
    from_y = exchange(piece, 4)
    own_twin = exchange(piece, 1)
    far_low = exchange(from_x[:half], 4)
    far_high = exchange(from_y[half:], 2)
    parts = [from_x, from_y, far_low, far_high]
    twins = [exchange(part, 1) for part in parts]
    return jnp.concatenate([piece, *parts, own_twin, *twins], axis=0)


def add_low(left, right):
    return (left.astype(jnp.float32) + right.astype(jnp.float32)).astype(jnp.bfloat16)


def scatter_rows(left, multiply):
    tp_count = lax.axis_size("tp")
    if tp_count != SWAP_TP:
        return lax.psum_scatter(multiply(left), "tp", scatter_dimension=0, tiled=True).astype(
            jnp.float32
        )
    rows = left.shape[0] // SWAP_TP
    half = rows // 2

    def both(first, count):
        twin = multiply(left[(4 + first) * rows : (4 + first + count) * rows])
        return add_low(multiply(left[first * rows : (first + count) * rows]), exchange(twin, 1))

    far = both(3, 1)
    far_low = exchange(far[:half], 2)
    far_high = exchange(far[half:], 4)
    mixed = both(1, 2)
    to_x, to_y = mixed[:rows], mixed[rows:]
    x_low = exchange(to_x[:half], 2)
    y_high = exchange(to_y[half:], 4)
    home = both(0, 1)
    x_high = exchange(add_low(to_x[half:], far_high), 2)
    y_low = exchange(add_low(to_y[:half], far_low), 4)
    wide = [part.astype(jnp.float32) for part in (x_low, x_high, y_low, y_high)]
    return (
        home.astype(jnp.float32)
        + jnp.concatenate(wide[:2], axis=0)
        + jnp.concatenate(wide[2:], axis=0)
    )


def sum_over(vector, axis):
    count = lax.axis_size(axis)
    terms = [vector] + [
        lax.ppermute(vector, axis, [(at, at ^ step) for at in range(count)])
        for step in range(1, count)
    ]
    while len(terms) > 1:
        terms = [terms[at] + terms[at + 1] for at in range(0, len(terms), 2)]
    return terms[0]


def block_table(seq_len, seq_group, group_id, block_count):
    seq_order = jnp.arange(seq_len.shape[0], dtype=jnp.int32)
    same_before = (seq_group[None, :] == seq_group[:, None]) & (
        seq_order[None, :] < seq_order[:, None]
    )
    starts = jnp.sum(jnp.where(same_before, seq_len[None, :], 0), axis=1) // BLOCK
    ends = starts + seq_len // BLOCK
    block_at = jnp.arange(block_count, dtype=jnp.int32)
    inside = (
        (seq_group[None, :] == group_id)
        & (starts[None, :] <= block_at[:, None])
        & (block_at[:, None] < ends[None, :])
    )
    held = jnp.sum(inside.astype(jnp.int32), axis=1)
    first = jnp.sum(jnp.where(inside, starts[None, :], 0), axis=1)
    first = jnp.where(held > 0, first, block_at)
    place = block_at
    if lax.axis_size("tp") == SWAP_TP:
        apart = block_at ^ lax.axis_index("tp")
        place = (apart >> 1) + 4 * (apart & 1)
    return jnp.stack([place, first, held]).astype(jnp.int32)


def dot_nt(left, right):
    return lax.dot_general(
        left, right, (((1,), (1,)), ((), ())), preferred_element_type=jnp.float32
    )


def block_rows(place):
    return pl.ds(pl.multiple_of(place * BLOCK, BLOCK), BLOCK)


def attend_kernel(table, qkv, ctx, lse):
    head_cols = ctx.shape[1]
    heads = head_cols // HEAD_DIM
    sharpness = HEAD_DIM ** (-0.5) * LOG2_E
    row_at = lax.broadcasted_iota(jnp.int32, (BLOCK, BLOCK), 0)
    col_at = lax.broadcasted_iota(jnp.int32, (BLOCK, BLOCK), 1)

    def cols(part, head):
        return pl.ds(part * head_cols + head * HEAD_DIM, HEAD_DIM)

    def query_block(at, _):
        rows = block_rows(table[0, at])
        queries = [qkv[rows, cols(0, head)] for head in range(heads)]
        allowed = (col_at == row_at) | ((col_at < row_at) & (table[2, at] > 0))

        def start(head):
            scores = dot_nt(queries[head], qkv[rows, cols(1, head)]) * sharpness
            scores = jnp.where(allowed, scores, MASKED)
            top = jnp.max(scores, axis=-1, keepdims=True)
            weights = jnp.exp2(scores - top)
            total = jnp.sum(weights, axis=-1, keepdims=True)
            mixed = jnp.dot(
                weights.astype(jnp.bfloat16),
                qkv[rows, cols(2, head)],
                preferred_element_type=jnp.float32,
            )
            return top, total, mixed

        def key_block(key_at, carried):
            key_rows = block_rows(table[0, key_at])
            result = []
            for head in range(heads):
                top, total, mixed = carried[head]
                scores = dot_nt(queries[head], qkv[key_rows, cols(1, head)]) * sharpness
                new_top = jnp.maximum(top, jnp.max(scores, axis=-1, keepdims=True))
                shrink = jnp.exp2(top - new_top)
                weights = jnp.exp2(scores - new_top)
                total = total * shrink + jnp.sum(weights, axis=-1, keepdims=True)
                mixed = mixed * shrink + jnp.dot(
                    weights.astype(jnp.bfloat16),
                    qkv[key_rows, cols(2, head)],
                    preferred_element_type=jnp.float32,
                )
                result.append((new_top, total, mixed))
            return tuple(result)

        done = lax.fori_loop(
            table[1, at], at, key_block, tuple(start(head) for head in range(heads))
        )
        for head in range(heads):
            top, total, mixed = done[head]
            ctx[rows, pl.ds(head * HEAD_DIM, HEAD_DIM)] = (mixed / total).astype(jnp.bfloat16)
            level = jnp.broadcast_to(top + jnp.log2(total), (BLOCK, HEAD_DIM))
            lse[pl.ds(head * 8, 8), rows] = level.T[:8]
        return 0

    lax.fori_loop(0, table.shape[1], query_block, 0)


def attend_back_kernel(table, qkv, ctx, ctx_grad, lse, qkv_grad, sums, key_acc, value_acc):
    head_cols = ctx.shape[1]
    heads = head_cols // HEAD_DIM
    scaling = HEAD_DIM ** (-0.5)
    sharpness = scaling * LOG2_E
    key_row = lax.broadcasted_iota(jnp.int32, (BLOCK, BLOCK), 0)
    query_col = lax.broadcasted_iota(jnp.int32, (BLOCK, BLOCK), 1)
    sums[...] = jnp.zeros_like(sums)

    def cols(part, head):
        return pl.ds(part * head_cols + head * HEAD_DIM, HEAD_DIM)

    def query_block(at, _):
        rows = block_rows(table[0, at])
        queries, grads, levels, dots = [], [], [], []
        for head in range(heads):
            own = pl.ds(head * HEAD_DIM, HEAD_DIM)
            queries.append(qkv[rows, cols(0, head)])
            grads.append(ctx_grad[rows, own])
            levels.append(lse[pl.ds(head * 8, 1), rows])
            dot = jnp.sum(
                grads[head].astype(jnp.float32) * ctx[rows, own].astype(jnp.float32),
                axis=-1,
                keepdims=True,
            )
            dots.append(jnp.broadcast_to(dot, (BLOCK, HEAD_DIM)).T[:1])
        allowed = (key_row == query_col) | ((key_row < query_col) & (table[2, at] > 0))

        def tile(head, key_rows, masked):
            keys = qkv[key_rows, cols(1, head)]
            probs = jnp.exp2(dot_nt(keys, queries[head]) * sharpness - levels[head])
            if masked:
                probs = jnp.where(allowed, probs, 0.0)
            prob_grad = dot_nt(qkv[key_rows, cols(2, head)], grads[head])
            score_grad = (probs * (prob_grad - dots[head])).astype(jnp.bfloat16)
            value_part = jnp.dot(
                probs.astype(jnp.bfloat16), grads[head], preferred_element_type=jnp.float32
            )
            key_part = jnp.dot(score_grad, queries[head], preferred_element_type=jnp.float32)
            return contract_rows(score_grad, keys), key_part, value_part

        query_acc = []
        for head in range(heads):
            own = pl.ds(head * HEAD_DIM, HEAD_DIM)
            query_part, key_part, value_part = tile(head, rows, True)
            key_acc[rows, own] = key_part
            value_acc[rows, own] = value_part
            query_acc.append(query_part)

        def key_block(key_at, carried):
            key_rows = block_rows(table[0, key_at])
            result = []
            for head in range(heads):
                own = pl.ds(head * HEAD_DIM, HEAD_DIM)
                query_part, key_part, value_part = tile(head, key_rows, False)
                key_acc[key_rows, own] += key_part
                value_acc[key_rows, own] += value_part
                result.append(carried[head] + query_part)
            return tuple(result)

        query_acc = lax.fori_loop(table[1, at], at, key_block, tuple(query_acc))
        for head in range(heads):
            low = (query_acc[head] * scaling).astype(jnp.bfloat16)
            qkv_grad[rows, cols(0, head)] = low
            sums[:1, pl.ds(head * HEAD_DIM, HEAD_DIM)] += jnp.sum(
                low.astype(jnp.float32), axis=0, keepdims=True
            )
        return 0

    lax.fori_loop(0, table.shape[1], query_block, 0)

    def finish(at, _):
        rows = block_rows(at)
        key_low = (key_acc[rows, :] * scaling).astype(jnp.bfloat16)
        value_low = value_acc[rows, :].astype(jnp.bfloat16)
        qkv_grad[rows, pl.ds(head_cols, head_cols)] = key_low
        qkv_grad[rows, pl.ds(2 * head_cols, head_cols)] = value_low
        sums[1:2, :] += jnp.sum(value_low.astype(jnp.float32), axis=0, keepdims=True)
        return 0

    lax.fori_loop(0, table.shape[1], finish, 0)


def whole_specs(count):
    return [pl.BlockSpec(memory_space=pltpu.VMEM) for _ in range(count)]


def attend(table, qkv_rows, head_cols):
    rows = qkv_rows.shape[0]
    heads = head_cols // HEAD_DIM
    return pl.pallas_call(
        attend_kernel,
        out_shape=(
            jax.ShapeDtypeStruct((rows, head_cols), jnp.bfloat16),
            jax.ShapeDtypeStruct((8 * heads, rows), jnp.float32),
        ),
        in_specs=[pl.BlockSpec(memory_space=pltpu.SMEM), *whole_specs(1)],
        out_specs=tuple(whole_specs(2)),
        name="attend",
    )(table, qkv_rows)


def attend_back(table, qkv_rows, context, ctx_grad, lse):
    rows, head_cols = context.shape
    return pl.pallas_call(
        attend_back_kernel,
        out_shape=(
            jax.ShapeDtypeStruct(qkv_rows.shape, jnp.bfloat16),
            jax.ShapeDtypeStruct((8, head_cols), jnp.float32),
        ),
        in_specs=[pl.BlockSpec(memory_space=pltpu.SMEM), *whole_specs(4)],
        out_specs=tuple(whole_specs(2)),
        scratch_shapes=[
            pltpu.VMEM((rows, head_cols), jnp.float32),
            pltpu.VMEM((rows, head_cols), jnp.float32),
        ],
        name="attend_back",
    )(table, qkv_rows, context, ctx_grad, lse)


def local(
    tokens,
    seq_len,
    seq_group,
    ln1_gain,
    ln1_bias,
    qkv_weight,
    qv_bias,
    out_weight,
    out_bias,
    ln2_gain,
    ln2_bias,
    up_weight,
    up_bias,
    down_weight,
    down_bias,
    out_grad,
):
    width = tokens.shape[1]
    head_cols = qkv_weight.shape[2]
    table = block_table(
        seq_len,
        seq_group,
        lax.axis_index("fsdp"),
        tokens.shape[0] * lax.axis_size("tp") // BLOCK,
    )

    def gather_weights():
        return (
            lax.all_gather(qkv_weight, "fsdp", axis=0, tiled=True),
            lax.all_gather(out_weight, "fsdp", axis=1, tiled=True),
            lax.all_gather(up_weight, "fsdp", axis=0, tiled=True),
            lax.all_gather(down_weight, "fsdp", axis=1, tiled=True),
        )

    inputs = tokens.astype(jnp.float32)
    norm1 = layer_norm(inputs, ln1_gain, ln1_bias).astype(jnp.bfloat16)
    qkv_full, out_full, up_full, down_full = gather_weights()
    qkv_flat = qkv_full.reshape(width, 3 * head_cols)
    qkv_shift = jnp.concatenate([qv_bias[0], jnp.zeros_like(qv_bias[0]), qv_bias[1]])
    norm1_rows = gather_rows(norm1)
    qkv_rows = (
        jnp.dot(
            norm1_rows,
            qkv_flat,
            preferred_element_type=jnp.float32,
        )
        + qkv_shift
    ).astype(jnp.bfloat16)
    out_grad, norm1_rows = lax.optimization_barrier((out_grad, norm1_rows))
    grad_piece = gather_rows(out_grad)
    context, lse = attend(table, qkv_rows, head_cols)
    context, grad_piece = lax.optimization_barrier((context, grad_piece))
    attn_rows = scatter_rows(
        context,
        lambda part: jnp.dot(part, out_full, preferred_element_type=jnp.float32).astype(
            jnp.bfloat16
        ),
    )
    middle = inputs + attn_rows + out_bias
    norm2 = layer_norm(middle, ln2_gain, ln2_bias).astype(jnp.bfloat16)
    norm_piece = gather_rows(norm2)
    pre = (
        jnp.dot(
            norm_piece,
            up_full,
            preferred_element_type=jnp.float32,
        )
        + up_bias
    )
    act_rows = gelu_tanh(pre).astype(jnp.bfloat16)
    mlp_rows = scatter_rows(
        act_rows,
        lambda part: jnp.dot(part, down_full, preferred_element_type=jnp.float32).astype(
            jnp.bfloat16
        ),
    )
    layer_out = (middle + mlp_rows + down_bias).astype(jnp.bfloat16)
    grad_rows = out_grad.astype(jnp.float32)
    act_value, gelu_back = jax.vjp(gelu_tanh, pre)
    act_piece = act_value.astype(jnp.bfloat16)
    down_acc = contract_rows(act_piece, grad_piece)
    act_grad = contract_cols(grad_piece, down_full)
    pre_grad = gelu_back(act_grad)[0].astype(jnp.bfloat16)
    up_acc = contract_rows(norm_piece, pre_grad)
    shift_acc = jnp.sum(pre_grad.astype(jnp.float32), axis=0)
    norm2_grad = scatter_rows(
        pre_grad, lambda part: contract_cols(part, up_full).astype(jnp.bfloat16)
    )
    unused_two, ln2_back = jax.vjp(layer_norm, middle, ln2_gain, ln2_bias)
    middle_ln, grad_g2, grad_b2 = ln2_back(norm2_grad)
    middle_grad = grad_rows + middle_ln
    proj_grad = middle_grad.astype(jnp.bfloat16)
    portion = gather_rows(proj_grad)
    out_acc = contract_rows(context, portion)
    ctx_grad = contract_cols(portion, out_full).astype(jnp.bfloat16)
    grad_out_w = out_acc
    qkv_grad, sums = attend_back(table, qkv_rows, context, ctx_grad, lse)
    early = sum_over(
        sum_over(
            jnp.stack([jnp.sum(middle_grad, axis=0), grad_g2, grad_b2, jnp.sum(grad_rows, axis=0)]),
            "fsdp",
        ),
        "tp",
    )
    qkv_grad, early = lax.optimization_barrier((qkv_grad, early))
    qv_sums = sums[:2]
    norm1_grad = scatter_rows(
        qkv_grad, lambda part: contract_cols(part, qkv_flat).astype(jnp.bfloat16)
    )
    unused_one, ln1_back = jax.vjp(layer_norm, inputs, ln1_gain, ln1_bias)
    input_ln, grad_g1, grad_b1 = ln1_back(norm1_grad)
    tokens_grad = (middle_grad + input_ln).astype(jnp.bfloat16)
    grad_qkv_flat = contract_rows(norm1_rows, qkv_grad)
    grad_qkv_w = grad_qkv_flat.reshape(width, 3, head_cols)
    shard_qkv, shard_out, shard_up, shard_down = (
        lax.psum_scatter(
            grad_qkv_w.astype(jnp.bfloat16), "fsdp", scatter_dimension=0, tiled=True
        ).astype(jnp.float32),
        lax.psum_scatter(
            grad_out_w.astype(jnp.bfloat16), "fsdp", scatter_dimension=1, tiled=True
        ).astype(jnp.float32),
        lax.psum_scatter(
            up_acc.astype(jnp.bfloat16), "fsdp", scatter_dimension=0, tiled=True
        ).astype(jnp.float32),
        lax.psum_scatter(
            down_acc.astype(jnp.bfloat16), "fsdp", scatter_dimension=1, tiled=True
        ).astype(jnp.float32),
    )
    own_sums = sum_over(jnp.concatenate([qv_sums.reshape(-1), shift_acc]), "fsdp")
    grad_qv = own_sums[: 2 * head_cols].reshape(2, head_cols)
    grad_upb_own = own_sums[2 * head_cols :]
    late = sum_over(sum_over(jnp.stack([grad_g1, grad_b1]), "fsdp"), "tp")
    return (
        layer_out,
        tokens_grad,
        late[0],
        late[1],
        shard_qkv,
        grad_qv,
        shard_out,
        early[0],
        early[1],
        early[2],
        shard_up,
        grad_upb_own,
        shard_down,
        early[3],
    )


def solution(mesh):
    placed = (
        P(("fsdp", "tp"), None),
        P(),
        P(),
        P(),
        P(),
        P("fsdp", None, "tp"),
        P(None, "tp"),
        P("tp", "fsdp"),
        P(),
        P(),
        P(),
        P("fsdp", "tp"),
        P("tp"),
        P("tp", "fsdp"),
        P(),
        P(("fsdp", "tp"), None),
    )
    return jax.shard_map(
        local,
        mesh=mesh,
        in_specs=placed,
        out_specs=(
            P(("fsdp", "tp"), None),
            P(("fsdp", "tp"), None),
            P(),
            P(),
            P("fsdp", None, "tp"),
            P(None, "tp"),
            P("tp", "fsdp"),
            P(),
            P(),
            P(),
            P("fsdp", "tp"),
            P("tp"),
            P("tp", "fsdp"),
            P(),
        ),
        check_vma=False,
    )
```

```python
import jax
import jax.numpy as jnp
from jax import lax
from jax.experimental import pallas as pl
from jax.experimental.pallas import tpu as pltpu
from jax.sharding import PartitionSpec as P

HEAD_DIM = 128


EPSILON = 1e-05
MASKED = -1e30


def layer_norm(values, gain_vec, bias_vec):
    row_mean = jnp.mean(values, axis=-1, keepdims=True)
    centred = values - row_mean
    variance = jnp.mean(centred * centred, axis=-1, keepdims=True)
    return centred * lax.rsqrt(variance + EPSILON) * gain_vec + bias_vec


def gelu_pair(values):
    squared = values * values
    bent = jnp.tanh(GELU_RATE * values * (1.0 + GELU_CUBE * squared))
    upper = 0.5 * (1.0 + bent)
    slope = upper + 0.5 * values * (1.0 - bent * bent) * GELU_RATE * (1.0 + 3.0 * GELU_CUBE * squared)
    return values * upper, slope


def contract_rows(left, right):
    return lax.dot_general(
        left, right, (((0,), (0,)), ((), ())), preferred_element_type=jnp.float32
    )


def contract_cols(left, right):
    return lax.dot_general(
        left, right, (((1,), (1,)), ((), ())), preferred_element_type=jnp.float32
    )


SWAP_TP = 8
BLOCK = 256
LOG2_E = 1.4426950408889634
GELU_RATE = 0.7978845608028654
GELU_CUBE = 0.044715


def exchange(piece, mask):
    return lax.ppermute(piece, "tp", [(at, at ^ mask) for at in range(SWAP_TP)])


def tie(*values):
    return lax.optimization_barrier(values)


def gather_first(piece):
    if lax.axis_size("tp") != SWAP_TP:
        return (lax.all_gather(piece, "tp", axis=0, tiled=True),)
    return piece, exchange(piece, 2), exchange(piece, 4), exchange(piece, 1)


def gather_second(state):
    if len(state) == 1:
        return state
    piece, from_x, from_y, own_twin = state
    half = piece.shape[0] // 2
    far_low = exchange(from_x[:half], 4)
    far_high = exchange(from_y[half:], 2)
    return piece, from_x, from_y, far_low, far_high, own_twin, exchange(from_x, 1), exchange(from_y, 1)


def gather_last(state):
    if len(state) == 1:
        return state[0]
    far_low, far_high = state[3:5]
    return jnp.concatenate([*state, exchange(far_low, 1), exchange(far_high, 1)], axis=0)


def gather_rows(piece):
    return gather_last(gather_second(gather_first(piece)))


def add_low(left, right):
    return (left.astype(jnp.float32) + right.astype(jnp.float32)).astype(jnp.bfloat16)


def scatter_multiply(left, multiply):
    if lax.axis_size("tp") != SWAP_TP:
        return (multiply(left),)
    rows = left.shape[0] // SWAP_TP

    def both(first, count):
        twin = multiply(left[(4 + first) * rows : (4 + first + count) * rows])
        return add_low(multiply(left[first * rows : (first + count) * rows]), exchange(twin, 1))

    return both(3, 1), both(1, 2), both(0, 1)


def scatter_first(parts):
    if len(parts) == 1:
        return (lax.psum_scatter(parts[0], "tp", scatter_dimension=0, tiled=True),)
    far, mixed, home = parts
    rows = far.shape[0]
    half = rows // 2
    to_x, to_y = mixed[:rows], mixed[rows:]
    return (
        exchange(far[:half], 2),
        exchange(far[half:], 4),
        exchange(to_x[:half], 2),
        exchange(to_y[half:], 4),
        to_x[half:],
        to_y[:half],
        home,
    )


def scatter_second(state):
    if len(state) == 1:
        return state
    far_low, far_high, x_low, y_high, to_x, to_y, home = state
    return (
        x_low,
        exchange(add_low(to_x, far_high), 2),
        exchange(add_low(to_y, far_low), 4),
        y_high,
        home,
    )


def scatter_last(state):
    if len(state) == 1:
        return state[0].astype(jnp.float32)
    x_low, x_high, y_low, y_high, home = (part.astype(jnp.float32) for part in state)
    return (
        home
        + jnp.concatenate([x_low, x_high], axis=0)
        + jnp.concatenate([y_low, y_high], axis=0)
    )


def sum_over(vector, axis):
    count = lax.axis_size(axis)
    terms = [vector] + [
        lax.ppermute(vector, axis, [(at, at ^ step) for at in range(count)])
        for step in range(1, count)
    ]
    while len(terms) > 1:
        terms = [terms[at] + terms[at + 1] for at in range(0, len(terms), 2)]
    return terms[0]


def block_table(seq_len, seq_group, group_id, block_count):
    seq_order = jnp.arange(seq_len.shape[0], dtype=jnp.int32)
    same_before = (seq_group[None, :] == seq_group[:, None]) & (
        seq_order[None, :] < seq_order[:, None]
    )
    starts = jnp.sum(jnp.where(same_before, seq_len[None, :], 0), axis=1) // BLOCK
    ends = starts + seq_len // BLOCK
    block_at = jnp.arange(block_count, dtype=jnp.int32)
    inside = (
        (seq_group[None, :] == group_id)
        & (starts[None, :] <= block_at[:, None])
        & (block_at[:, None] < ends[None, :])
    )
    held = jnp.sum(inside.astype(jnp.int32), axis=1)
    first = jnp.sum(jnp.where(inside, starts[None, :], 0), axis=1)
    first = jnp.where(held > 0, first, block_at)
    place = block_at
    if lax.axis_size("tp") == SWAP_TP:
        apart = block_at ^ lax.axis_index("tp")
        place = (apart >> 1) + 4 * (apart & 1)
    return jnp.stack([place, first, held]).astype(jnp.int32)


def dot_nt(left, right):
    return lax.dot_general(
        left, right, (((1,), (1,)), ((), ())), preferred_element_type=jnp.float32
    )


def block_rows(place):
    return pl.ds(pl.multiple_of(place * BLOCK, BLOCK), BLOCK)


def attend_kernel(table, qkv, ctx, lse):
    head_cols = ctx.shape[1]
    heads = head_cols // HEAD_DIM
    sharpness = HEAD_DIM ** (-0.5) * LOG2_E
    row_at = lax.broadcasted_iota(jnp.int32, (BLOCK, BLOCK), 0)
    col_at = lax.broadcasted_iota(jnp.int32, (BLOCK, BLOCK), 1)

    def cols(part, head):
        return pl.ds(part * head_cols + head * HEAD_DIM, HEAD_DIM)

    def query_block(at, _):
        rows = block_rows(table[0, at])
        queries = [qkv[rows, cols(0, head)] for head in range(heads)]
        allowed = (col_at == row_at) | ((col_at < row_at) & (table[2, at] > 0))

        def start(head):
            scores = dot_nt(queries[head], qkv[rows, cols(1, head)]) * sharpness
            scores = jnp.where(allowed, scores, MASKED)
            top = jnp.max(scores, axis=-1, keepdims=True)
            weights = jnp.exp2(scores - top)
            total = jnp.sum(weights, axis=-1, keepdims=True)
            mixed = jnp.dot(
                weights.astype(jnp.bfloat16),
                qkv[rows, cols(2, head)],
                preferred_element_type=jnp.float32,
            )
            return top, total, mixed

        def key_block(key_at, carried):
            key_rows = block_rows(table[0, key_at])
            result = []
            for head in range(heads):
                top, total, mixed = carried[head]
                scores = dot_nt(queries[head], qkv[key_rows, cols(1, head)]) * sharpness
                new_top = jnp.maximum(top, jnp.max(scores, axis=-1, keepdims=True))
                shrink = jnp.exp2(top - new_top)
                weights = jnp.exp2(scores - new_top)
                total = total * shrink + jnp.sum(weights, axis=-1, keepdims=True)
                mixed = mixed * shrink + jnp.dot(
                    weights.astype(jnp.bfloat16),
                    qkv[key_rows, cols(2, head)],
                    preferred_element_type=jnp.float32,
                )
                result.append((new_top, total, mixed))
            return tuple(result)

        done = lax.fori_loop(
            table[1, at], at, key_block, tuple(start(head) for head in range(heads))
        )
        for head in range(heads):
            top, total, mixed = done[head]
            ctx[rows, pl.ds(head * HEAD_DIM, HEAD_DIM)] = (mixed / total).astype(jnp.bfloat16)
            level = jnp.broadcast_to(top + jnp.log2(total), (BLOCK, HEAD_DIM))
            lse[pl.ds(head * 8, 8), rows] = level.T[:8]
        return 0

    lax.fori_loop(0, table.shape[1], query_block, 0)


def attend_back_kernel(table, qkv, ctx, ctx_grad, lse, qkv_grad, sums, key_acc, value_acc):
    head_cols = ctx.shape[1]
    heads = head_cols // HEAD_DIM
    scaling = HEAD_DIM ** (-0.5)
    sharpness = scaling * LOG2_E
    key_row = lax.broadcasted_iota(jnp.int32, (BLOCK, BLOCK), 0)
    query_col = lax.broadcasted_iota(jnp.int32, (BLOCK, BLOCK), 1)
    sums[...] = jnp.zeros_like(sums)

    def cols(part, head):
        return pl.ds(part * head_cols + head * HEAD_DIM, HEAD_DIM)

    def query_block(at, _):
        rows = block_rows(table[0, at])
        queries, grads, levels, dots = [], [], [], []
        for head in range(heads):
            own = pl.ds(head * HEAD_DIM, HEAD_DIM)
            queries.append(qkv[rows, cols(0, head)])
            grads.append(ctx_grad[rows, own])
            levels.append(lse[pl.ds(head * 8, 1), rows])
            dot = jnp.sum(
                grads[head].astype(jnp.float32) * ctx[rows, own].astype(jnp.float32),
                axis=-1,
                keepdims=True,
            )
            dots.append(jnp.broadcast_to(dot, (BLOCK, HEAD_DIM)).T[:1])
        allowed = (key_row == query_col) | ((key_row < query_col) & (table[2, at] > 0))

        def tile(head, key_rows, masked):
            keys = qkv[key_rows, cols(1, head)]
            probs = jnp.exp2(dot_nt(keys, queries[head]) * sharpness - levels[head])
            if masked:
                probs = jnp.where(allowed, probs, 0.0)
            prob_grad = dot_nt(qkv[key_rows, cols(2, head)], grads[head])
            score_grad = (probs * (prob_grad - dots[head])).astype(jnp.bfloat16)
            value_part = jnp.dot(
                probs.astype(jnp.bfloat16), grads[head], preferred_element_type=jnp.float32
            )
            key_part = jnp.dot(score_grad, queries[head], preferred_element_type=jnp.float32)
            return contract_rows(score_grad, keys), key_part, value_part

        query_acc = []
        for head in range(heads):
            own = pl.ds(head * HEAD_DIM, HEAD_DIM)
            query_part, key_part, value_part = tile(head, rows, True)
            key_acc[rows, own] = key_part
            value_acc[rows, own] = value_part
            query_acc.append(query_part)

        def key_block(key_at, carried):
            key_rows = block_rows(table[0, key_at])
            result = []
            for head in range(heads):
                own = pl.ds(head * HEAD_DIM, HEAD_DIM)
                query_part, key_part, value_part = tile(head, key_rows, False)
                key_acc[key_rows, own] += key_part
                value_acc[key_rows, own] += value_part
                result.append(carried[head] + query_part)
            return tuple(result)

        query_acc = lax.fori_loop(table[1, at], at, key_block, tuple(query_acc))
        for head in range(heads):
            low = (query_acc[head] * scaling).astype(jnp.bfloat16)
            qkv_grad[rows, cols(0, head)] = low
            sums[:1, pl.ds(head * HEAD_DIM, HEAD_DIM)] += jnp.sum(
                low.astype(jnp.float32), axis=0, keepdims=True
            )
        return 0

    lax.fori_loop(0, table.shape[1], query_block, 0)

    def finish(at, _):
        rows = block_rows(at)
        key_low = (key_acc[rows, :] * scaling).astype(jnp.bfloat16)
        value_low = value_acc[rows, :].astype(jnp.bfloat16)
        qkv_grad[rows, pl.ds(head_cols, head_cols)] = key_low
        qkv_grad[rows, pl.ds(2 * head_cols, head_cols)] = value_low
        sums[1:2, :] += jnp.sum(value_low.astype(jnp.float32), axis=0, keepdims=True)
        return 0

    lax.fori_loop(0, table.shape[1], finish, 0)


def whole_specs(count):
    return [pl.BlockSpec(memory_space=pltpu.VMEM) for _ in range(count)]


def attend(table, qkv_rows, head_cols):
    rows = qkv_rows.shape[0]
    heads = head_cols // HEAD_DIM
    return pl.pallas_call(
        attend_kernel,
        out_shape=(
            jax.ShapeDtypeStruct((rows, head_cols), jnp.bfloat16),
            jax.ShapeDtypeStruct((8 * heads, rows), jnp.float32),
        ),
        in_specs=[pl.BlockSpec(memory_space=pltpu.SMEM), *whole_specs(1)],
        out_specs=tuple(whole_specs(2)),
        name="attend",
    )(table, qkv_rows)


def attend_back(table, qkv_rows, context, ctx_grad, lse):
    rows, head_cols = context.shape
    return pl.pallas_call(
        attend_back_kernel,
        out_shape=(
            jax.ShapeDtypeStruct(qkv_rows.shape, jnp.bfloat16),
            jax.ShapeDtypeStruct((8, head_cols), jnp.float32),
        ),
        in_specs=[pl.BlockSpec(memory_space=pltpu.SMEM), *whole_specs(4)],
        out_specs=tuple(whole_specs(2)),
        scratch_shapes=[
            pltpu.VMEM((rows, head_cols), jnp.float32),
            pltpu.VMEM((rows, head_cols), jnp.float32),
        ],
        name="attend_back",
    )(table, qkv_rows, context, ctx_grad, lse)


def local(
    tokens,
    seq_len,
    seq_group,
    ln1_gain,
    ln1_bias,
    qkv_weight,
    qv_bias,
    out_weight,
    out_bias,
    ln2_gain,
    ln2_bias,
    up_weight,
    up_bias,
    down_weight,
    down_bias,
    out_grad,
):
    width = tokens.shape[1]
    head_cols = qkv_weight.shape[2]
    table = block_table(
        seq_len,
        seq_group,
        lax.axis_index("fsdp"),
        tokens.shape[0] * lax.axis_size("tp") // BLOCK,
    )

    def gather_weights():
        return (
            lax.all_gather(qkv_weight, "fsdp", axis=0, tiled=True),
            lax.all_gather(out_weight, "fsdp", axis=1, tiled=True),
            lax.all_gather(up_weight, "fsdp", axis=0, tiled=True),
            lax.all_gather(down_weight, "fsdp", axis=1, tiled=True),
        )

    inputs = tokens.astype(jnp.float32)
    norm1 = layer_norm(inputs, ln1_gain, ln1_bias).astype(jnp.bfloat16)
    qkv_full, out_full, up_full, down_full = gather_weights()
    qkv_flat = qkv_full.reshape(width, 3 * head_cols)
    qkv_shift = jnp.concatenate([qv_bias[0], jnp.zeros_like(qv_bias[0]), qv_bias[1]])
    norm1_rows = gather_rows(norm1)
    later_grad, norm1_rows = tie(out_grad, norm1_rows)
    grad_state = gather_first(later_grad)
    qkv_rows = (
        jnp.dot(norm1_rows, qkv_flat, preferred_element_type=jnp.float32) + qkv_shift
    ).astype(jnp.bfloat16)
    grad_state, qkv_rows = tie(grad_state, qkv_rows)
    grad_state = gather_second(grad_state)
    context, lse = attend(table, qkv_rows, head_cols)
    grad_state, context = tie(grad_state, context)

    attn_parts = scatter_multiply(
        context,
        lambda part: jnp.dot(part, out_full, preferred_element_type=jnp.float32).astype(
            jnp.bfloat16
        ),
    )
    attn_rows = scatter_last(scatter_second(scatter_first(attn_parts)))
    middle = inputs + attn_rows + out_bias
    norm2 = layer_norm(middle, ln2_gain, ln2_bias).astype(jnp.bfloat16)
    norm2_state = gather_first(norm2)
    grad_state, norm2_state = tie(grad_state, norm2_state)
    grad_piece = gather_last(grad_state)
    norm_piece = gather_last(gather_second(norm2_state))
    pre = jnp.dot(norm_piece, up_full, preferred_element_type=jnp.float32) + up_bias
    act_value, slope = gelu_pair(pre)
    act_rows, slope = tie(act_value.astype(jnp.bfloat16), slope.astype(jnp.bfloat16))

    down_acc = contract_rows(act_rows, grad_piece).astype(jnp.bfloat16)
    down_full, down_acc = tie(down_full, down_acc)
    act_grad = contract_cols(grad_piece, down_full)
    pre_grad = (act_grad * slope.astype(jnp.float32)).astype(jnp.bfloat16)
    shift_acc = jnp.sum(pre_grad.astype(jnp.float32), axis=0)
    norm2_grad_state = scatter_first(
        scatter_multiply(
            pre_grad, lambda part: contract_cols(part, up_full).astype(jnp.bfloat16)
        )
    )
    up_acc = contract_rows(norm_piece, pre_grad).astype(jnp.bfloat16)
    norm2_grad_state, up_acc = tie(norm2_grad_state, up_acc)
    norm2_grad = scatter_last(scatter_second(norm2_grad_state))
    unused_two, ln2_back = jax.vjp(layer_norm, middle, ln2_gain, ln2_bias)
    middle_ln, grad_g2, grad_b2 = ln2_back(norm2_grad)
    grad_rows = out_grad.astype(jnp.float32)
    middle_grad = grad_rows + middle_ln
    proj_grad, act_rows = tie(middle_grad.astype(jnp.bfloat16), act_rows)
    portion_state = gather_first(proj_grad)
    mlp_parts = scatter_multiply(
        act_rows,
        lambda part: jnp.dot(part, down_full, preferred_element_type=jnp.float32).astype(
            jnp.bfloat16
        ),
    )
    portion_state, mlp_parts = tie(portion_state, mlp_parts)
    portion = gather_last(gather_second(portion_state))
    portion, mlp_parts = tie(portion, mlp_parts)
    mlp_state = scatter_first(mlp_parts)
    ctx_grad = contract_cols(portion, out_full).astype(jnp.bfloat16)
    out_acc = contract_rows(context, portion).astype(jnp.bfloat16)
    out_acc, ctx_grad = tie(out_acc, ctx_grad)
    qkv_grad, qv_sums = attend_back(table, qkv_rows, context, ctx_grad, lse)
    mlp_state, qkv_grad = tie(mlp_state, qkv_grad)
    mlp_rows = scatter_last(scatter_second(mlp_state))
    layer_out = (middle + mlp_rows + down_bias).astype(jnp.bfloat16)

    norm1_grad_state = scatter_first(
        scatter_multiply(
            qkv_grad, lambda part: contract_cols(part, qkv_flat).astype(jnp.bfloat16)
        )
    )
    grad_qkv_w = contract_rows(norm1_rows, qkv_grad).astype(jnp.bfloat16)
    norm1_grad_state, grad_qkv_w = tie(norm1_grad_state, grad_qkv_w)
    norm1_grad = scatter_last(scatter_second(norm1_grad_state))
    unused_one, ln1_back = jax.vjp(layer_norm, inputs, ln1_gain, ln1_bias)
    input_ln, grad_g1, grad_b1 = ln1_back(norm1_grad)
    tokens_grad = (middle_grad + input_ln).astype(jnp.bfloat16)

    def sum_weights(partial_sums, axis):
        return lax.psum_scatter(
            partial_sums, "fsdp", scatter_dimension=axis, tiled=True
        ).astype(jnp.float32)

    shard_down = sum_weights(down_acc, 1)
    shard_up = sum_weights(up_acc, 0)
    shard_out = sum_weights(out_acc, 1)
    shard_qkv = sum_weights(grad_qkv_w.reshape(width, 3, head_cols), 0)
    wide_sums = [
        jnp.sum(middle_grad, axis=0),
        grad_g2,
        grad_b2,
        jnp.sum(grad_rows, axis=0),
        grad_g1,
        grad_b1,
    ]
    summed = sum_over(
        jnp.concatenate([*wide_sums, qv_sums[0], qv_sums[1], shift_acc]), "fsdp"
    )
    wide = sum_over(summed[: 6 * width], "tp").reshape(6, width)
    own = summed[6 * width :]
    return (
        layer_out,
        tokens_grad,
        wide[4],
        wide[5],
        shard_qkv,
        own[: 2 * head_cols].reshape(2, head_cols),
        shard_out,
        wide[0],
        wide[1],
        wide[2],
        shard_up,
        own[2 * head_cols :],
        shard_down,
        wide[3],
    )


def solution(mesh):
    placed = (
        P(("fsdp", "tp"), None),
        P(),
        P(),
        P(),
        P(),
        P("fsdp", None, "tp"),
        P(None, "tp"),
        P("tp", "fsdp"),
        P(),
        P(),
        P(),
        P("fsdp", "tp"),
        P("tp"),
        P("tp", "fsdp"),
        P(),
        P(("fsdp", "tp"), None),
    )
    return jax.shard_map(
        local,
        mesh=mesh,
        in_specs=placed,
        out_specs=(
            P(("fsdp", "tp"), None),
            P(("fsdp", "tp"), None),
            P(),
            P(),
            P("fsdp", None, "tp"),
            P(None, "tp"),
            P("tp", "fsdp"),
            P(),
            P(),
            P(),
            P("fsdp", "tp"),
            P("tp"),
            P("tp", "fsdp"),
            P(),
        ),
        check_vma=False,
    )
```

```python
import jax
import jax.numpy as jnp
from jax import lax
from jax.experimental import pallas as pl
from jax.experimental.pallas import tpu as pltpu
from jax.sharding import PartitionSpec as P

HEAD_DIM = 128


EPSILON = 1e-05
MASKED = -1e30


def layer_norm(values, gain_vec, bias_vec):
    row_mean = jnp.mean(values, axis=-1, keepdims=True)
    centred = values - row_mean
    variance = jnp.mean(centred * centred, axis=-1, keepdims=True)
    return centred * lax.rsqrt(variance + EPSILON) * gain_vec + bias_vec


def gelu_pair(values):
    squared = values * values
    bent = jnp.tanh(GELU_RATE * values * (1.0 + GELU_CUBE * squared))
    upper = 0.5 * (1.0 + bent)
    slope = upper + 0.5 * values * (1.0 - bent * bent) * GELU_RATE * (1.0 + 3.0 * GELU_CUBE * squared)
    return values * upper, slope


def contract_rows(left, right):
    return lax.dot_general(
        left, right, (((0,), (0,)), ((), ())), preferred_element_type=jnp.float32
    )


def contract_cols(left, right):
    return lax.dot_general(
        left, right, (((1,), (1,)), ((), ())), preferred_element_type=jnp.float32
    )


SWAP_TP = 8
BLOCK = 256
LOG2_E = 1.4426950408889634
GELU_RATE = 0.7978845608028654
GELU_CUBE = 0.044715


def exchange(piece, mask):
    return lax.ppermute(piece, "tp", [(at, at ^ mask) for at in range(SWAP_TP)])


def tie(*values):
    return lax.optimization_barrier(values)


def gather_first(piece):
    if lax.axis_size("tp") != SWAP_TP:
        return (lax.all_gather(piece, "tp", axis=0, tiled=True),)
    return piece, exchange(piece, 2), exchange(piece, 4), exchange(piece, 1)


def gather_second(state):
    if len(state) == 1:
        return state
    piece, from_x, from_y, own_twin = state
    half = piece.shape[0] // 2
    far_low = exchange(from_x[:half], 4)
    far_high = exchange(from_y[half:], 2)
    return piece, from_x, from_y, far_low, far_high, own_twin, exchange(from_x, 1), exchange(from_y, 1)


def gather_last(state):
    if len(state) == 1:
        return state[0]
    far_low, far_high = state[3:5]
    return jnp.concatenate([*state, exchange(far_low, 1), exchange(far_high, 1)], axis=0)


def gather_rows(piece):
    return gather_last(gather_second(gather_first(piece)))


def add_low(left, right):
    return (left.astype(jnp.float32) + right.astype(jnp.float32)).astype(jnp.bfloat16)


def scatter_pair(left, multiply, first, count):
    if lax.axis_size("tp") != SWAP_TP:
        return multiply(left)
    rows = left.shape[0] // SWAP_TP
    twin = multiply(left[(4 + first) * rows : (4 + first + count) * rows])
    return add_low(multiply(left[first * rows : (first + count) * rows]), exchange(twin, 1))


def scatter_multiply(left, multiply):
    if lax.axis_size("tp") != SWAP_TP:
        return (scatter_pair(left, multiply, 0, 0),)
    return tuple(scatter_pair(left, multiply, first, count) for first, count in ((3, 1), (1, 2), (0, 1)))


def scatter_first(parts):
    if len(parts) == 1:
        return (lax.psum_scatter(parts[0], "tp", scatter_dimension=0, tiled=True),)
    far, mixed, home = parts
    rows = far.shape[0]
    half = rows // 2
    to_x, to_y = mixed[:rows], mixed[rows:]
    return (
        exchange(far[:half], 2),
        exchange(far[half:], 4),
        exchange(to_x[:half], 2),
        exchange(to_y[half:], 4),
        to_x[half:],
        to_y[:half],
        home,
    )


def scatter_second(state):
    if len(state) == 1:
        return state
    far_low, far_high, x_low, y_high, to_x, to_y, home = state
    return (
        x_low,
        exchange(add_low(to_x, far_high), 2),
        exchange(add_low(to_y, far_low), 4),
        y_high,
        home,
    )


def scatter_last(state):
    if len(state) == 1:
        return state[0].astype(jnp.float32)
    x_low, x_high, y_low, y_high, home = (part.astype(jnp.float32) for part in state)
    return (
        home
        + jnp.concatenate([x_low, x_high], axis=0)
        + jnp.concatenate([y_low, y_high], axis=0)
    )


def sum_over(vector, axis):
    count = lax.axis_size(axis)
    terms = [vector] + [
        lax.ppermute(vector, axis, [(at, at ^ step) for at in range(count)])
        for step in range(1, count)
    ]
    while len(terms) > 1:
        terms = [terms[at] + terms[at + 1] for at in range(0, len(terms), 2)]
    return terms[0]


def block_table(seq_len, seq_group, group_id, block_count):
    seq_order = jnp.arange(seq_len.shape[0], dtype=jnp.int32)
    same_before = (seq_group[None, :] == seq_group[:, None]) & (
        seq_order[None, :] < seq_order[:, None]
    )
    starts = jnp.sum(jnp.where(same_before, seq_len[None, :], 0), axis=1) // BLOCK
    ends = starts + seq_len // BLOCK
    block_at = jnp.arange(block_count, dtype=jnp.int32)
    inside = (
        (seq_group[None, :] == group_id)
        & (starts[None, :] <= block_at[:, None])
        & (block_at[:, None] < ends[None, :])
    )
    held = jnp.sum(inside.astype(jnp.int32), axis=1)
    first = jnp.sum(jnp.where(inside, starts[None, :], 0), axis=1)
    first = jnp.where(held > 0, first, block_at)
    place = block_at
    if lax.axis_size("tp") == SWAP_TP:
        apart = block_at ^ lax.axis_index("tp")
        place = (apart >> 1) + 4 * (apart & 1)
    return jnp.stack([place, first, held]).astype(jnp.int32)


def dot_nt(left, right):
    return lax.dot_general(
        left, right, (((1,), (1,)), ((), ())), preferred_element_type=jnp.float32
    )


def block_rows(place):
    return pl.ds(pl.multiple_of(place * BLOCK, BLOCK), BLOCK)


def attend_kernel(table, qkv, ctx, lse):
    head_cols = ctx.shape[1]
    heads = head_cols // HEAD_DIM
    sharpness = HEAD_DIM ** (-0.5) * LOG2_E
    key_row = lax.broadcasted_iota(jnp.int32, (BLOCK, BLOCK), 0)
    query_col = lax.broadcasted_iota(jnp.int32, (BLOCK, BLOCK), 1)

    def cols(part, head):
        return pl.ds(part * head_cols + head * HEAD_DIM, HEAD_DIM)

    def query_block(at, _):
        rows = block_rows(table[0, at])
        queries = [qkv[rows, cols(0, head)] for head in range(heads)]
        allowed = (key_row == query_col) | ((key_row < query_col) & (table[2, at] > 0))

        def start(head):
            scores = dot_nt(qkv[rows, cols(1, head)], queries[head]) * sharpness
            scores = jnp.where(allowed, scores, MASKED)
            top = jnp.max(scores, axis=0, keepdims=True)
            weights = jnp.exp2(scores - top)
            total = jnp.sum(weights, axis=0, keepdims=True)
            return top, total, contract_rows(qkv[rows, cols(2, head)], weights.astype(jnp.bfloat16))

        def key_block(key_at, carried):
            key_rows = block_rows(table[0, key_at])
            result = []
            for head in range(heads):
                top, total, mixed = carried[head]
                scores = dot_nt(qkv[key_rows, cols(1, head)], queries[head]) * sharpness
                new_top = jnp.maximum(top, jnp.max(scores, axis=0, keepdims=True))
                shrink = jnp.exp2(top - new_top)
                weights = jnp.exp2(scores - new_top)
                total = total * shrink + jnp.sum(weights, axis=0, keepdims=True)
                mixed = mixed * shrink + contract_rows(
                    qkv[key_rows, cols(2, head)], weights.astype(jnp.bfloat16)
                )
                result.append((new_top, total, mixed))
            return tuple(result)

        done = lax.fori_loop(
            table[1, at], at, key_block, tuple(start(head) for head in range(heads))
        )
        for head in range(heads):
            top, total, mixed = done[head]
            ctx[rows, pl.ds(head * HEAD_DIM, HEAD_DIM)] = (mixed / total).T.astype(jnp.bfloat16)
            lse[pl.ds(head * 8, 8), rows] = jnp.broadcast_to(top + jnp.log2(total), (8, BLOCK))
        return 0

    lax.fori_loop(0, table.shape[1], query_block, 0)


def attend_back_kernel(table, qkv, ctx, ctx_grad, lse, qkv_grad, sums, key_acc, value_acc):
    head_cols = ctx.shape[1]
    heads = head_cols // HEAD_DIM
    scaling = HEAD_DIM ** (-0.5)
    sharpness = scaling * LOG2_E
    key_row = lax.broadcasted_iota(jnp.int32, (BLOCK, BLOCK), 0)
    query_col = lax.broadcasted_iota(jnp.int32, (BLOCK, BLOCK), 1)
    sums[...] = jnp.zeros_like(sums)

    def cols(part, head):
        return pl.ds(part * head_cols + head * HEAD_DIM, HEAD_DIM)

    def query_block(at, _):
        rows = block_rows(table[0, at])
        queries, grads, levels, dots = [], [], [], []
        for head in range(heads):
            own = pl.ds(head * HEAD_DIM, HEAD_DIM)
            queries.append(qkv[rows, cols(0, head)])
            grads.append(ctx_grad[rows, own])
            levels.append(lse[pl.ds(head * 8, 1), rows])
            dot = jnp.sum(
                grads[head].astype(jnp.float32) * ctx[rows, own].astype(jnp.float32),
                axis=-1,
                keepdims=True,
            )
            dots.append(jnp.broadcast_to(dot, (BLOCK, HEAD_DIM)).T[:1])
        allowed = (key_row == query_col) | ((key_row < query_col) & (table[2, at] > 0))

        def tile(head, key_rows, masked):
            keys = qkv[key_rows, cols(1, head)]
            probs = jnp.exp2(dot_nt(keys, queries[head]) * sharpness - levels[head])
            if masked:
                probs = jnp.where(allowed, probs, 0.0)
            prob_grad = dot_nt(qkv[key_rows, cols(2, head)], grads[head])
            score_grad = (probs * (prob_grad - dots[head])).astype(jnp.bfloat16)
            value_part = jnp.dot(
                probs.astype(jnp.bfloat16), grads[head], preferred_element_type=jnp.float32
            )
            key_part = jnp.dot(score_grad, queries[head], preferred_element_type=jnp.float32)
            return contract_rows(score_grad, keys), key_part, value_part

        query_acc = []
        for head in range(heads):
            own = pl.ds(head * HEAD_DIM, HEAD_DIM)
            query_part, key_part, value_part = tile(head, rows, True)
            key_acc[rows, own] = key_part
            value_acc[rows, own] = value_part
            query_acc.append(query_part)

        def key_block(key_at, carried):
            key_rows = block_rows(table[0, key_at])
            result = []
            for head in range(heads):
                own = pl.ds(head * HEAD_DIM, HEAD_DIM)
                query_part, key_part, value_part = tile(head, key_rows, False)
                key_acc[key_rows, own] += key_part
                value_acc[key_rows, own] += value_part
                result.append(carried[head] + query_part)
            return tuple(result)

        query_acc = lax.fori_loop(table[1, at], at, key_block, tuple(query_acc))
        for head in range(heads):
            low = (query_acc[head] * scaling).astype(jnp.bfloat16)
            qkv_grad[rows, cols(0, head)] = low
            sums[:1, pl.ds(head * HEAD_DIM, HEAD_DIM)] += jnp.sum(
                low.astype(jnp.float32), axis=0, keepdims=True
            )
        return 0

    lax.fori_loop(0, table.shape[1], query_block, 0)

    def finish(at, _):
        rows = block_rows(at)
        key_low = (key_acc[rows, :] * scaling).astype(jnp.bfloat16)
        value_low = value_acc[rows, :].astype(jnp.bfloat16)
        qkv_grad[rows, pl.ds(head_cols, head_cols)] = key_low
        qkv_grad[rows, pl.ds(2 * head_cols, head_cols)] = value_low
        sums[1:2, :] += jnp.sum(value_low.astype(jnp.float32), axis=0, keepdims=True)
        return 0

    lax.fori_loop(0, table.shape[1], finish, 0)


def whole_specs(count):
    return [pl.BlockSpec(memory_space=pltpu.VMEM) for _ in range(count)]


def attend(table, qkv_rows, head_cols):
    rows = qkv_rows.shape[0]
    heads = head_cols // HEAD_DIM
    return pl.pallas_call(
        attend_kernel,
        out_shape=(
            jax.ShapeDtypeStruct((rows, head_cols), jnp.bfloat16),
            jax.ShapeDtypeStruct((8 * heads, rows), jnp.float32),
        ),
        in_specs=[pl.BlockSpec(memory_space=pltpu.SMEM), *whole_specs(1)],
        out_specs=tuple(whole_specs(2)),
        name="attend",
    )(table, qkv_rows)


def attend_back(table, qkv_rows, context, ctx_grad, lse):
    rows, head_cols = context.shape
    return pl.pallas_call(
        attend_back_kernel,
        out_shape=(
            jax.ShapeDtypeStruct(qkv_rows.shape, jnp.bfloat16),
            jax.ShapeDtypeStruct((8, head_cols), jnp.float32),
        ),
        in_specs=[pl.BlockSpec(memory_space=pltpu.SMEM), *whole_specs(4)],
        out_specs=tuple(whole_specs(2)),
        scratch_shapes=[
            pltpu.VMEM((rows, head_cols), jnp.float32),
            pltpu.VMEM((rows, head_cols), jnp.float32),
        ],
        name="attend_back",
    )(table, qkv_rows, context, ctx_grad, lse)


def local(
    tokens,
    seq_len,
    seq_group,
    ln1_gain,
    ln1_bias,
    qkv_weight,
    qv_bias,
    out_weight,
    out_bias,
    ln2_gain,
    ln2_bias,
    up_weight,
    up_bias,
    down_weight,
    down_bias,
    out_grad,
):
    width = tokens.shape[1]
    head_cols = qkv_weight.shape[2]
    table = block_table(
        seq_len,
        seq_group,
        lax.axis_index("fsdp"),
        tokens.shape[0] * lax.axis_size("tp") // BLOCK,
    )

    def gather_weights():
        return (
            lax.all_gather(qkv_weight, "fsdp", axis=0, tiled=True),
            lax.all_gather(out_weight, "fsdp", axis=1, tiled=True),
            lax.all_gather(up_weight, "fsdp", axis=0, tiled=True),
            lax.all_gather(down_weight, "fsdp", axis=1, tiled=True),
        )

    def sum_weights(partial_sums, axis):
        return lax.psum_scatter(
            partial_sums, "fsdp", scatter_dimension=axis, tiled=True
        )

    inputs = tokens.astype(jnp.float32)
    norm1 = layer_norm(inputs, ln1_gain, ln1_bias).astype(jnp.bfloat16)
    qkv_full, out_full, up_full, down_full = gather_weights()
    qkv_flat = qkv_full.reshape(width, 3 * head_cols)
    qkv_shift = jnp.concatenate([qv_bias[0], jnp.zeros_like(qv_bias[0]), qv_bias[1]])
    norm1_rows = gather_rows(norm1)
    later_grad, norm1_rows = tie(out_grad, norm1_rows)
    grad_state = gather_first(later_grad)
    qkv_rows = (
        jnp.dot(norm1_rows, qkv_flat, preferred_element_type=jnp.float32) + qkv_shift
    ).astype(jnp.bfloat16)
    grad_state, qkv_rows = tie(grad_state, qkv_rows)
    grad_state = gather_second(grad_state)
    context, lse = attend(table, qkv_rows, head_cols)
    grad_state, context = tie(grad_state, context)

    attn_parts = scatter_multiply(
        context,
        lambda part: jnp.dot(part, out_full, preferred_element_type=jnp.float32).astype(
            jnp.bfloat16
        ),
    )
    attn_rows = scatter_last(scatter_second(scatter_first(attn_parts)))
    middle = inputs + attn_rows + out_bias
    norm2 = layer_norm(middle, ln2_gain, ln2_bias).astype(jnp.bfloat16)
    norm2_state = gather_first(norm2)
    grad_piece, norm2_state = tie(gather_last(grad_state), norm2_state)
    norm_piece = gather_last(gather_second(norm2_state))
    pre = jnp.dot(norm_piece, up_full, preferred_element_type=jnp.float32) + up_bias
    act_value, slope = gelu_pair(pre)
    act_rows, slope = tie(act_value.astype(jnp.bfloat16), slope.astype(jnp.bfloat16))

    down_acc = contract_rows(act_rows, grad_piece).astype(jnp.bfloat16)
    down_full, down_acc = tie(down_full, down_acc)
    act_grad = contract_cols(grad_piece, down_full)
    pre_grad = (act_grad * slope.astype(jnp.float32)).astype(jnp.bfloat16)
    shift_acc = jnp.sum(pre_grad.astype(jnp.float32), axis=0)
    norm2_grad_state = scatter_first(
        scatter_multiply(
            pre_grad, lambda part: contract_cols(part, up_full).astype(jnp.bfloat16)
        )
    )
    up_acc = contract_rows(norm_piece, pre_grad).astype(jnp.bfloat16)
    norm2_grad_state, up_acc = tie(norm2_grad_state, up_acc)
    norm2_grad = scatter_last(scatter_second(norm2_grad_state))
    unused_two, ln2_back = jax.vjp(layer_norm, middle, ln2_gain, ln2_bias)
    middle_ln, grad_g2, grad_b2 = ln2_back(norm2_grad)
    grad_rows = out_grad.astype(jnp.float32)
    middle_grad = grad_rows + middle_ln
    proj_grad, act_rows = tie(middle_grad.astype(jnp.bfloat16), act_rows)
    portion_state = gather_first(proj_grad)
    mlp_parts = scatter_multiply(
        act_rows,
        lambda part: jnp.dot(part, down_full, preferred_element_type=jnp.float32).astype(
            jnp.bfloat16
        ),
    )
    portion_state, mlp_parts = tie(portion_state, mlp_parts)
    portion = gather_last(gather_second(portion_state))
    portion, mlp_parts = tie(portion, mlp_parts)
    mlp_state = scatter_first(mlp_parts)
    shard_down = sum_weights(down_acc, 1)
    portion, shard_down = tie(portion, shard_down)
    ctx_grad = contract_cols(portion, out_full).astype(jnp.bfloat16)
    out_acc = contract_rows(context, portion).astype(jnp.bfloat16)
    out_acc, ctx_grad = tie(out_acc, ctx_grad)
    qkv_grad, qv_sums = attend_back(table, qkv_rows, context, ctx_grad, lse)
    mlp_state, qkv_grad = tie(mlp_state, qkv_grad)
    mlp_rows = scatter_last(scatter_second(mlp_state))
    layer_out = (middle + mlp_rows + down_bias).astype(jnp.bfloat16)

    shard_up = sum_weights(up_acc, 0)
    shard_out = sum_weights(out_acc, 1)

    def norm1_multiply(part):
        return contract_cols(part, qkv_flat).astype(jnp.bfloat16)

    norm1_far = scatter_pair(qkv_grad, norm1_multiply, 3, 1)
    norm1_far, qkv_grad = tie(norm1_far, qkv_grad)
    grad_qkv_w = contract_rows(norm1_rows, qkv_grad).astype(jnp.bfloat16)
    grad_qkv_w, qkv_grad, shard_up = tie(grad_qkv_w, qkv_grad, shard_up)
    norm1_state = scatter_first(
        (
            norm1_far,
            scatter_pair(qkv_grad, norm1_multiply, 1, 2),
            scatter_pair(qkv_grad, norm1_multiply, 0, 1),
        )
        if lax.axis_size("tp") == SWAP_TP
        else (norm1_far,)
    )
    norm1_state, shard_out = tie(norm1_state, shard_out)
    norm1_grad = scatter_last(scatter_second(norm1_state))
    shard_qkv = sum_weights(grad_qkv_w.reshape(width, 3, head_cols), 0)
    unused_one, ln1_back = jax.vjp(layer_norm, inputs, ln1_gain, ln1_bias)
    input_ln, grad_g1, grad_b1 = ln1_back(norm1_grad)
    tokens_grad = (middle_grad + input_ln).astype(jnp.bfloat16)

    wide_sums = [
        jnp.sum(middle_grad, axis=0),
        grad_g2,
        grad_b2,
        jnp.sum(grad_rows, axis=0),
        grad_g1,
        grad_b1,
    ]
    summed = sum_over(
        jnp.concatenate([*wide_sums, qv_sums[0], qv_sums[1], shift_acc]), "fsdp"
    )
    wide = sum_over(summed[: 6 * width], "tp").reshape(6, width)
    own = summed[6 * width :]
    return (
        layer_out,
        tokens_grad,
        wide[4],
        wide[5],
        shard_qkv.astype(jnp.float32),
        own[: 2 * head_cols].reshape(2, head_cols),
        shard_out.astype(jnp.float32),
        wide[0],
        wide[1],
        wide[2],
        shard_up.astype(jnp.float32),
        own[2 * head_cols :],
        shard_down.astype(jnp.float32),
        wide[3],
    )


def solution(mesh):
    placed = (
        P(("fsdp", "tp"), None),
        P(),
        P(),
        P(),
        P(),
        P("fsdp", None, "tp"),
        P(None, "tp"),
        P("tp", "fsdp"),
        P(),
        P(),
        P(),
        P("fsdp", "tp"),
        P("tp"),
        P("tp", "fsdp"),
        P(),
        P(("fsdp", "tp"), None),
    )
    return jax.shard_map(
        local,
        mesh=mesh,
        in_specs=placed,
        out_specs=(
            P(("fsdp", "tp"), None),
            P(("fsdp", "tp"), None),
            P(),
            P(),
            P("fsdp", None, "tp"),
            P(None, "tp"),
            P("tp", "fsdp"),
            P(),
            P(),
            P(),
            P("fsdp", "tp"),
            P("tp"),
            P("tp", "fsdp"),
            P(),
        ),
        check_vma=False,
    )
```

```python
import jax
import jax.numpy as jnp
from jax import lax
from jax.experimental import pallas as pl
from jax.experimental.pallas import tpu as pltpu
from jax.sharding import PartitionSpec as P

HEAD_DIM = 128


EPSILON = 1e-05
MASKED = -1e30


def layer_norm(values, gain_vec, bias_vec):
    row_mean = jnp.mean(values, axis=-1, keepdims=True)
    centred = values - row_mean
    variance = jnp.mean(centred * centred, axis=-1, keepdims=True)
    return centred * lax.rsqrt(variance + EPSILON) * gain_vec + bias_vec


def gelu_pair(values):
    squared = values * values
    bent = jnp.tanh(GELU_RATE * values * (1.0 + GELU_CUBE * squared))
    upper = 0.5 * (1.0 + bent)
    slope = upper + 0.5 * values * (1.0 - bent * bent) * GELU_RATE * (1.0 + 3.0 * GELU_CUBE * squared)
    return values * upper, slope


def contract_rows(left, right):
    return lax.dot_general(
        left, right, (((0,), (0,)), ((), ())), preferred_element_type=jnp.float32
    )


def contract_cols(left, right):
    return lax.dot_general(
        left, right, (((1,), (1,)), ((), ())), preferred_element_type=jnp.float32
    )


SWAP_TP = 8
BLOCK = 256
LOG2_E = 1.4426950408889634
GELU_RATE = 0.7978845608028654
GELU_CUBE = 0.044715


def exchange(piece, mask):
    return lax.ppermute(piece, "tp", [(at, at ^ mask) for at in range(SWAP_TP)])


def tie(*values):
    return lax.optimization_barrier(values)


def gather_first(piece):
    if lax.axis_size("tp") != SWAP_TP:
        return (lax.all_gather(piece, "tp", axis=0, tiled=True),)
    half = piece.shape[0] // 2
    low, high = piece[:half], piece[half:]
    x_low, y_high = exchange(low, 2), exchange(high, 4)
    x_high, y_low = exchange(high, 2), exchange(low, 4)
    return low, high, x_low, x_high, y_low, y_high, exchange(low, 1), exchange(high, 1)


def gather_second(state):
    if len(state) == 1:
        return state
    low, high, x_low, x_high, y_low, y_high, *own_twin = state
    far_low, far_high = exchange(x_low, 4), exchange(y_high, 2)
    near = (x_low, x_high, y_low, y_high)
    return (low, high, *near, far_low, far_high, *own_twin, *(exchange(part, 1) for part in near))


def gather_last(state):
    if len(state) == 1:
        return state[0]
    far_low, far_high = state[6:8]
    return jnp.concatenate([*state, exchange(far_low, 1), exchange(far_high, 1)], axis=0)


def gather_rows(piece):
    return gather_last(gather_second(gather_first(piece)))


def add_low(left, right):
    return (left.astype(jnp.float32) + right.astype(jnp.float32)).astype(jnp.bfloat16)


def scatter_pair(left, multiply, first, count):
    rows = left.shape[0] // SWAP_TP
    half = rows // 2
    twin = exchange(multiply(left[(4 + first) * rows : (4 + first + count) * rows]), 1)
    own = multiply(left[first * rows : (first + count) * rows])
    return tuple(
        add_low(own[at : at + half], twin[at : at + half]) for at in range(0, count * rows, half)
    )


def scatter_multiply(left, multiply):
    if lax.axis_size("tp") != SWAP_TP:
        return (multiply(left),)
    return sum((scatter_pair(left, multiply, *span) for span in ((3, 1), (1, 2), (0, 1))), ())


def scatter_first(parts):
    if len(parts) == 1:
        return (lax.psum_scatter(parts[0], "tp", scatter_dimension=0, tiled=True),)
    far_low, far_high, x_low, x_high, y_low, y_high, *home = parts
    return (
        exchange(far_low, 2),
        exchange(far_high, 4),
        exchange(x_low, 2),
        exchange(y_high, 4),
        x_high,
        y_low,
        *home,
    )


def scatter_second(state):
    if len(state) == 1:
        return state
    far_low, far_high, x_low, y_high, to_x, to_y, *home = state
    x_high = exchange(add_low(to_x, far_high), 2)
    y_low = exchange(add_low(to_y, far_low), 4)
    return x_low, x_high, y_low, y_high, *home


def scatter_last(state):
    if len(state) == 1:
        return state[0].astype(jnp.float32)
    x_low, x_high, y_low, y_high, low, high = (part.astype(jnp.float32) for part in state)
    return jnp.concatenate([low + x_low + y_low, high + x_high + y_high], axis=0)


def shift_fsdp(piece, step):
    count = lax.axis_size("fsdp")
    return lax.ppermute(piece, "fsdp", [(at, (at + step) % count) for at in range(count)])


def spread_fsdp(piece, axis):
    count, own, width = lax.axis_size("fsdp"), lax.axis_index("fsdp"), piece.shape[axis]
    shape = list(piece.shape)
    shape[axis] = width * count
    full = jnp.zeros(shape, piece.dtype)
    for step in range(count):
        part = shift_fsdp(piece, step) if step else piece
        full = lax.dynamic_update_slice_in_dim(full, part, (own - step) % count * width, axis)
    return full


def collect_fsdp(partial_sums, axis):
    count, own = lax.axis_size("fsdp"), lax.axis_index("fsdp")
    width = partial_sums.shape[axis] // count
    total = 0.0
    for step in range(count):
        part = lax.dynamic_slice_in_dim(partial_sums, (own + step) % count * width, width, axis)
        total = total + (shift_fsdp(part, step) if step else part).astype(jnp.float32)
    return total


def sum_direct(vector, axis, steps):
    count = lax.axis_size(axis)
    terms = [vector] + [
        lax.ppermute(vector, axis, [(at, at ^ step) for at in range(count)]) for step in steps
    ]
    while len(terms) > 1:
        terms = [terms[at] + terms[at + 1] for at in range(0, len(terms), 2)]
    return terms[0]


def sum_fsdp(vector):
    return sum_direct(vector, "fsdp", range(1, lax.axis_size("fsdp")))


def sum_tp(vector):
    return sum_direct(
        sum_direct(vector, "tp", (1,)), "tp", range(2, lax.axis_size("tp"), 2)
    )


def block_table(seq_len, seq_group, group_id, block_count):
    seq_order = jnp.arange(seq_len.shape[0], dtype=jnp.int32)
    same_before = (seq_group[None, :] == seq_group[:, None]) & (
        seq_order[None, :] < seq_order[:, None]
    )
    starts = jnp.sum(jnp.where(same_before, seq_len[None, :], 0), axis=1) // BLOCK
    ends = starts + seq_len // BLOCK
    block_at = jnp.arange(block_count, dtype=jnp.int32)
    inside = (
        (seq_group[None, :] == group_id)
        & (starts[None, :] <= block_at[:, None])
        & (block_at[:, None] < ends[None, :])
    )
    held = jnp.sum(inside.astype(jnp.int32), axis=1)
    first = jnp.sum(jnp.where(inside, starts[None, :], 0), axis=1)
    first = jnp.where(held > 0, first, block_at)
    place = block_at
    if lax.axis_size("tp") == SWAP_TP:
        apart = block_at ^ lax.axis_index("tp")
        place = (apart >> 1) + 4 * (apart & 1)
    return jnp.stack([place, first, held]).astype(jnp.int32)


def dot_nt(left, right):
    return lax.dot_general(
        left, right, (((1,), (1,)), ((), ())), preferred_element_type=jnp.float32
    )


def block_rows(place):
    return pl.ds(pl.multiple_of(place * BLOCK, BLOCK), BLOCK)


def attend_kernel(table, qkv, ctx, lse):
    head_cols = ctx.shape[1]
    heads = head_cols // HEAD_DIM
    sharpness = HEAD_DIM ** (-0.5) * LOG2_E
    key_row = lax.broadcasted_iota(jnp.int32, (BLOCK, BLOCK), 0)
    query_col = lax.broadcasted_iota(jnp.int32, (BLOCK, BLOCK), 1)

    def cols(part, head):
        return pl.ds(part * head_cols + head * HEAD_DIM, HEAD_DIM)

    def query_block(at, _):
        rows = block_rows(table[0, at])
        queries = [qkv[rows, cols(0, head)] for head in range(heads)]
        allowed = (key_row == query_col) | ((key_row < query_col) & (table[2, at] > 0))

        def start(head):
            scores = dot_nt(qkv[rows, cols(1, head)], queries[head]) * sharpness
            scores = jnp.where(allowed, scores, MASKED)
            top = jnp.max(scores, axis=0, keepdims=True)
            weights = jnp.exp2(scores - top)
            total = jnp.sum(weights, axis=0, keepdims=True)
            return top, total, contract_rows(qkv[rows, cols(2, head)], weights.astype(jnp.bfloat16))

        def key_block(key_at, carried):
            key_rows = block_rows(table[0, key_at])
            result = []
            for head in range(heads):
                top, total, mixed = carried[head]
                scores = dot_nt(qkv[key_rows, cols(1, head)], queries[head]) * sharpness
                new_top = jnp.maximum(top, jnp.max(scores, axis=0, keepdims=True))
                shrink = jnp.exp2(top - new_top)
                weights = jnp.exp2(scores - new_top)
                total = total * shrink + jnp.sum(weights, axis=0, keepdims=True)
                mixed = mixed * shrink + contract_rows(
                    qkv[key_rows, cols(2, head)], weights.astype(jnp.bfloat16)
                )
                result.append((new_top, total, mixed))
            return tuple(result)

        done = lax.fori_loop(
            table[1, at], at, key_block, tuple(start(head) for head in range(heads))
        )
        for head in range(heads):
            top, total, mixed = done[head]
            ctx[rows, pl.ds(head * HEAD_DIM, HEAD_DIM)] = (mixed / total).T.astype(jnp.bfloat16)
            lse[pl.ds(head * 8, 8), rows] = jnp.broadcast_to(top + jnp.log2(total), (8, BLOCK))
        return 0

    lax.fori_loop(0, table.shape[1], query_block, 0)


def attend_back_kernel(table, qkv, ctx, ctx_grad, lse, qkv_grad, sums, key_acc, value_acc):
    head_cols = ctx.shape[1]
    heads = head_cols // HEAD_DIM
    scaling = HEAD_DIM ** (-0.5)
    sharpness = scaling * LOG2_E
    key_row = lax.broadcasted_iota(jnp.int32, (BLOCK, BLOCK), 0)
    query_col = lax.broadcasted_iota(jnp.int32, (BLOCK, BLOCK), 1)
    sums[...] = jnp.zeros_like(sums)

    def cols(part, head):
        return pl.ds(part * head_cols + head * HEAD_DIM, HEAD_DIM)

    def query_block(at, _):
        rows = block_rows(table[0, at])
        queries, grads, levels, dots = [], [], [], []
        for head in range(heads):
            own = pl.ds(head * HEAD_DIM, HEAD_DIM)
            queries.append(qkv[rows, cols(0, head)])
            grads.append(ctx_grad[rows, own])
            levels.append(lse[pl.ds(head * 8, 1), rows])
            dot = jnp.sum(
                grads[head].astype(jnp.float32) * ctx[rows, own].astype(jnp.float32),
                axis=-1,
                keepdims=True,
            )
            dots.append(jnp.broadcast_to(dot, (BLOCK, HEAD_DIM)).T[:1])
        allowed = (key_row == query_col) | ((key_row < query_col) & (table[2, at] > 0))

        def tile(head, key_rows, masked):
            keys = qkv[key_rows, cols(1, head)]
            probs = jnp.exp2(dot_nt(keys, queries[head]) * sharpness - levels[head])
            if masked:
                probs = jnp.where(allowed, probs, 0.0)
            prob_grad = dot_nt(qkv[key_rows, cols(2, head)], grads[head])
            score_grad = (probs * (prob_grad - dots[head])).astype(jnp.bfloat16)
            value_part = jnp.dot(
                probs.astype(jnp.bfloat16), grads[head], preferred_element_type=jnp.float32
            )
            key_part = jnp.dot(score_grad, queries[head], preferred_element_type=jnp.float32)
            return contract_rows(score_grad, keys), key_part, value_part

        query_acc = []
        for head in range(heads):
            own = pl.ds(head * HEAD_DIM, HEAD_DIM)
            query_part, key_part, value_part = tile(head, rows, True)
            key_acc[rows, own] = key_part
            value_acc[rows, own] = value_part
            query_acc.append(query_part)

        def key_block(key_at, carried):
            key_rows = block_rows(table[0, key_at])
            result = []
            for head in range(heads):
                own = pl.ds(head * HEAD_DIM, HEAD_DIM)
                query_part, key_part, value_part = tile(head, key_rows, False)
                key_acc[key_rows, own] += key_part
                value_acc[key_rows, own] += value_part
                result.append(carried[head] + query_part)
            return tuple(result)

        query_acc = lax.fori_loop(table[1, at], at, key_block, tuple(query_acc))
        for head in range(heads):
            low = (query_acc[head] * scaling).astype(jnp.bfloat16)
            qkv_grad[rows, cols(0, head)] = low
            sums[:1, pl.ds(head * HEAD_DIM, HEAD_DIM)] += jnp.sum(
                low.astype(jnp.float32), axis=0, keepdims=True
            )
        return 0

    lax.fori_loop(0, table.shape[1], query_block, 0)

    def finish(at, _):
        rows = block_rows(at)
        key_low = (key_acc[rows, :] * scaling).astype(jnp.bfloat16)
        value_low = value_acc[rows, :].astype(jnp.bfloat16)
        qkv_grad[rows, pl.ds(head_cols, head_cols)] = key_low
        qkv_grad[rows, pl.ds(2 * head_cols, head_cols)] = value_low
        sums[1:2, :] += jnp.sum(value_low.astype(jnp.float32), axis=0, keepdims=True)
        return 0

    lax.fori_loop(0, table.shape[1], finish, 0)


def whole_specs(count):
    return [pl.BlockSpec(memory_space=pltpu.VMEM) for _ in range(count)]


def attend(table, qkv_rows, head_cols):
    rows = qkv_rows.shape[0]
    heads = head_cols // HEAD_DIM
    return pl.pallas_call(
        attend_kernel,
        out_shape=(
            jax.ShapeDtypeStruct((rows, head_cols), jnp.bfloat16),
            jax.ShapeDtypeStruct((8 * heads, rows), jnp.float32),
        ),
        in_specs=[pl.BlockSpec(memory_space=pltpu.SMEM), *whole_specs(1)],
        out_specs=tuple(whole_specs(2)),
        name="attend",
    )(table, qkv_rows)


def attend_back(table, qkv_rows, context, ctx_grad, lse):
    rows, head_cols = context.shape
    return pl.pallas_call(
        attend_back_kernel,
        out_shape=(
            jax.ShapeDtypeStruct(qkv_rows.shape, jnp.bfloat16),
            jax.ShapeDtypeStruct((8, head_cols), jnp.float32),
        ),
        in_specs=[pl.BlockSpec(memory_space=pltpu.SMEM), *whole_specs(4)],
        out_specs=tuple(whole_specs(2)),
        scratch_shapes=[
            pltpu.VMEM((rows, head_cols), jnp.float32),
            pltpu.VMEM((rows, head_cols), jnp.float32),
        ],
        name="attend_back",
    )(table, qkv_rows, context, ctx_grad, lse)


def local(
    tokens,
    seq_len,
    seq_group,
    ln1_gain,
    ln1_bias,
    qkv_weight,
    qv_bias,
    out_weight,
    out_bias,
    ln2_gain,
    ln2_bias,
    up_weight,
    up_bias,
    down_weight,
    down_bias,
    out_grad,
):
    width = tokens.shape[1]
    head_cols = qkv_weight.shape[2]
    table = block_table(
        seq_len,
        seq_group,
        lax.axis_index("fsdp"),
        tokens.shape[0] * lax.axis_size("tp") // BLOCK,
    )

    def gather_weights():
        return (
            lax.all_gather(qkv_weight, "fsdp", axis=0, tiled=True),
            lax.all_gather(up_weight, "fsdp", axis=0, tiled=True),
            lax.all_gather(down_weight, "fsdp", axis=1, tiled=True),
        )

    def sum_weights(partial_sums, axis):
        return lax.psum_scatter(
            partial_sums, "fsdp", scatter_dimension=axis, tiled=True
        )

    inputs = tokens.astype(jnp.float32)
    norm1 = layer_norm(inputs, ln1_gain, ln1_bias).astype(jnp.bfloat16)
    qkv_full, up_full, down_full = gather_weights()
    qkv_flat = qkv_full.reshape(width, 3 * head_cols)
    qkv_shift = jnp.concatenate([qv_bias[0], jnp.zeros_like(qv_bias[0]), qv_bias[1]])
    norm1_rows = gather_rows(norm1)
    later_grad, later_out, norm1_rows = tie(out_grad, out_weight, norm1_rows)
    out_full = spread_fsdp(later_out, 1)
    grad_state = gather_first(later_grad)
    qkv_rows = (
        jnp.dot(norm1_rows, qkv_flat, preferred_element_type=jnp.float32) + qkv_shift
    ).astype(jnp.bfloat16)
    grad_state, qkv_rows = tie(grad_state, qkv_rows)
    grad_state = gather_second(grad_state)
    context, lse = attend(table, qkv_rows, head_cols)
    grad_state, context = tie(grad_state, context)

    attn_parts = scatter_multiply(
        context,
        lambda part: jnp.dot(part, out_full, preferred_element_type=jnp.float32).astype(
            jnp.bfloat16
        ),
    )
    attn_rows = scatter_last(scatter_second(scatter_first(attn_parts)))
    middle = inputs + attn_rows + out_bias
    norm2 = layer_norm(middle, ln2_gain, ln2_bias).astype(jnp.bfloat16)
    norm2_state = gather_first(norm2)
    grad_piece, norm2_state = tie(gather_last(grad_state), norm2_state)
    norm_piece = gather_last(gather_second(norm2_state))
    pre = jnp.dot(norm_piece, up_full, preferred_element_type=jnp.float32) + up_bias
    act_value, slope = gelu_pair(pre)
    act_rows, slope = tie(act_value.astype(jnp.bfloat16), slope.astype(jnp.bfloat16))

    down_acc = contract_rows(act_rows, grad_piece).astype(jnp.bfloat16)
    down_full, down_acc = tie(down_full, down_acc)
    act_grad = contract_cols(grad_piece, down_full)
    pre_grad = (act_grad * slope.astype(jnp.float32)).astype(jnp.bfloat16)
    shift_acc = jnp.sum(pre_grad.astype(jnp.float32), axis=0)
    norm2_grad_state = scatter_first(
        scatter_multiply(
            pre_grad, lambda part: contract_cols(part, up_full).astype(jnp.bfloat16)
        )
    )
    up_acc = contract_rows(norm_piece, pre_grad).astype(jnp.bfloat16)
    norm2_grad_state, up_acc = tie(norm2_grad_state, up_acc)
    norm2_grad = scatter_last(scatter_second(norm2_grad_state))
    unused_two, ln2_back = jax.vjp(layer_norm, middle, ln2_gain, ln2_bias)
    middle_ln, grad_g2, grad_b2 = ln2_back(norm2_grad)
    grad_rows = out_grad.astype(jnp.float32)
    middle_grad = grad_rows + middle_ln
    portion_state = gather_first(middle_grad.astype(jnp.bfloat16))
    last_part, act_rows = tie(portion_state[-1], act_rows)
    portion_state = (*portion_state[:-1], last_part)
    mlp_parts = scatter_multiply(
        act_rows,
        lambda part: jnp.dot(part, down_full, preferred_element_type=jnp.float32).astype(
            jnp.bfloat16
        ),
    )
    portion_state, mlp_parts = tie(portion_state, mlp_parts)
    portion = gather_last(gather_second(portion_state))
    portion, mlp_parts = tie(portion, mlp_parts)
    mlp_state = scatter_first(mlp_parts)
    shard_down = sum_weights(down_acc, 1)
    early = jnp.concatenate(
        [jnp.sum(middle_grad, axis=0), grad_g2, grad_b2, jnp.sum(grad_rows, axis=0)]
    )
    early = sum_fsdp(jnp.concatenate([early, shift_acc]))
    grad_up_bias = early[4 * width :]
    early = sum_tp(early[: 4 * width]).reshape(4, width)
    portion, shard_down, early = tie(portion, shard_down, early)
    ctx_grad = contract_cols(portion, out_full).astype(jnp.bfloat16)
    qkv_grad, qv_sums = attend_back(table, qkv_rows, context, ctx_grad, lse)
    mlp_state, qkv_grad = tie(mlp_state, qkv_grad)
    mlp_state = scatter_second(mlp_state)

    shard_up = sum_weights(up_acc, 0)

    def norm1_multiply(part):
        return contract_cols(part, qkv_flat).astype(jnp.bfloat16)

    split = lax.axis_size("tp") == SWAP_TP
    norm1_parts = (
        scatter_pair(qkv_grad, norm1_multiply, 3, 1)
        if split
        else scatter_multiply(qkv_grad, norm1_multiply)
    )
    norm1_parts, qkv_grad = tie(norm1_parts, qkv_grad)
    grad_qkv_w = contract_rows(norm1_rows, qkv_grad).astype(jnp.bfloat16)
    grad_qkv_w, qkv_grad, shard_up, mlp_state = tie(grad_qkv_w, qkv_grad, shard_up, mlp_state)
    if split:
        norm1_parts = (
            *norm1_parts,
            *scatter_pair(qkv_grad, norm1_multiply, 1, 2),
            *scatter_pair(qkv_grad, norm1_multiply, 0, 1),
        )
    norm1_state = scatter_first(norm1_parts)
    layer_out = (middle + scatter_last(mlp_state) + down_bias).astype(jnp.bfloat16)
    out_acc = contract_rows(context, portion).astype(jnp.bfloat16)
    norm1_state, out_acc, layer_out = tie(norm1_state, out_acc, layer_out)
    norm1_state = scatter_second(norm1_state)
    shard_out = collect_fsdp(out_acc, 1)
    norm1_grad = scatter_last(norm1_state)
    shard_qkv = sum_weights(grad_qkv_w.reshape(width, 3, head_cols), 0)
    unused_one, ln1_back = jax.vjp(layer_norm, inputs, ln1_gain, ln1_bias)
    input_ln, grad_g1, grad_b1 = ln1_back(norm1_grad)
    tokens_grad = (middle_grad + input_ln).astype(jnp.bfloat16)

    late = sum_fsdp(jnp.concatenate([grad_g1, grad_b1, qv_sums[0], qv_sums[1]]))
    grad_qv = late[2 * width :].reshape(2, head_cols)
    late = sum_tp(late[: 2 * width]).reshape(2, width)
    return (
        layer_out,
        tokens_grad,
        late[0],
        late[1],
        shard_qkv.astype(jnp.float32),
        grad_qv,
        shard_out,
        early[0],
        early[1],
        early[2],
        shard_up.astype(jnp.float32),
        grad_up_bias,
        shard_down.astype(jnp.float32),
        early[3],
    )


def solution(mesh):
    placed = (
        P(("fsdp", "tp"), None),
        P(),
        P(),
        P(),
        P(),
        P("fsdp", None, "tp"),
        P(None, "tp"),
        P("tp", "fsdp"),
        P(),
        P(),
        P(),
        P("fsdp", "tp"),
        P("tp"),
        P("tp", "fsdp"),
        P(),
        P(("fsdp", "tp"), None),
    )
    return jax.shard_map(
        local,
        mesh=mesh,
        in_specs=placed,
        out_specs=(
            P(("fsdp", "tp"), None),
            P(("fsdp", "tp"), None),
            P(),
            P(),
            P("fsdp", None, "tp"),
            P(None, "tp"),
            P("tp", "fsdp"),
            P(),
            P(),
            P(),
            P("fsdp", "tp"),
            P("tp"),
            P("tp", "fsdp"),
            P(),
        ),
        check_vma=False,
    )
```

```python
import jax
import jax.numpy as jnp
from jax import lax
from jax.experimental import pallas as pl
from jax.experimental.pallas import tpu as pltpu
from jax.sharding import PartitionSpec as P

HEAD_DIM = 128


EPSILON = 1e-05
MASKED = -1e30


def layer_norm(values, gain_vec, bias_vec):
    row_mean = jnp.mean(values, axis=-1, keepdims=True)
    centred = values - row_mean
    variance = jnp.mean(centred * centred, axis=-1, keepdims=True)
    return centred * lax.rsqrt(variance + EPSILON) * gain_vec + bias_vec


def gelu_pair(values):
    squared = values * values
    bent = jnp.tanh(GELU_RATE * values * (1.0 + GELU_CUBE * squared))
    upper = 0.5 * (1.0 + bent)
    slope = upper + 0.5 * values * (1.0 - bent * bent) * GELU_RATE * (1.0 + 3.0 * GELU_CUBE * squared)
    return values * upper, slope


def contract_rows(left, right):
    return lax.dot_general(
        left, right, (((0,), (0,)), ((), ())), preferred_element_type=jnp.float32
    )


def contract_cols(left, right):
    return lax.dot_general(
        left, right, (((1,), (1,)), ((), ())), preferred_element_type=jnp.float32
    )


SWAP_TP = 8
BLOCK = 256
LOG2_E = 1.4426950408889634
GELU_RATE = 0.7978845608028654
GELU_CUBE = 0.044715


def exchange(piece, mask):
    return lax.ppermute(piece, "tp", [(at, at ^ mask) for at in range(SWAP_TP)])


def tie(*values):
    return lax.optimization_barrier(values)


def gather_first(piece):
    if lax.axis_size("tp") != SWAP_TP:
        return (lax.all_gather(piece, "tp", axis=0, tiled=True),)
    return piece, exchange(piece, 2), exchange(piece, 4), exchange(piece, 1)


def gather_second(state):
    if len(state) == 1:
        return state
    piece, from_x, from_y, own_twin = state
    half = piece.shape[0] // 2
    far_low = exchange(from_x[:half], 4)
    far_high = exchange(from_y[half:], 2)
    return piece, from_x, from_y, far_low, far_high, own_twin, exchange(from_x, 1), exchange(from_y, 1)


def gather_last(state):
    if len(state) == 1:
        return state[0]
    far_low, far_high = state[3:5]
    return jnp.concatenate([*state, exchange(far_low, 1), exchange(far_high, 1)], axis=0)


def gather_rows(piece):
    return gather_last(gather_second(gather_first(piece)))


def add_low(left, right):
    return (left.astype(jnp.float32) + right.astype(jnp.float32)).astype(jnp.bfloat16)


def scatter_pair(left, multiply, first, count):
    if lax.axis_size("tp") != SWAP_TP:
        return multiply(left)
    rows = left.shape[0] // SWAP_TP
    twin = multiply(left[(4 + first) * rows : (4 + first + count) * rows])
    return add_low(multiply(left[first * rows : (first + count) * rows]), exchange(twin, 1))


def scatter_multiply(left, multiply):
    if lax.axis_size("tp") != SWAP_TP:
        return (scatter_pair(left, multiply, 0, 0),)
    return tuple(scatter_pair(left, multiply, first, count) for first, count in ((3, 1), (1, 2), (0, 1)))


def scatter_pieces(parts):
    if len(parts) == 1:
        return parts
    far, mixed, home = parts
    rows = far.shape[0]
    half = rows // 2
    to_x, to_y = mixed[:rows], mixed[rows:]
    return far[:half], far[half:], to_x[:half], to_y[half:], to_x[half:], to_y[:half], home


def scatter_send(pieces):
    if len(pieces) == 1:
        return (lax.psum_scatter(pieces[0], "tp", scatter_dimension=0, tiled=True),)
    far_low, far_high, x_low, y_high, *kept = pieces
    return (
        exchange(far_low, 2),
        exchange(far_high, 4),
        exchange(x_low, 2),
        exchange(y_high, 4),
        *kept,
    )


def scatter_first(parts):
    return scatter_send(scatter_pieces(parts))


def scatter_second(state):
    if len(state) == 1:
        return state
    far_low, far_high, x_low, y_high, to_x, to_y, home = state
    return (
        x_low,
        exchange(add_low(to_x, far_high), 2),
        exchange(add_low(to_y, far_low), 4),
        y_high,
        home,
    )


def scatter_last(state):
    if len(state) == 1:
        return state[0].astype(jnp.float32)
    x_low, x_high, y_low, y_high, home = (part.astype(jnp.float32) for part in state)
    return (
        home
        + jnp.concatenate([x_low, x_high], axis=0)
        + jnp.concatenate([y_low, y_high], axis=0)
    )


def sum_direct(vector, axis, steps):
    count = lax.axis_size(axis)
    terms = [vector] + [
        lax.ppermute(vector, axis, [(at, at ^ step) for at in range(count)]) for step in steps
    ]
    while len(terms) > 1:
        terms = [terms[at] + terms[at + 1] for at in range(0, len(terms), 2)]
    return terms[0]


def sum_fsdp(vector):
    return sum_direct(vector, "fsdp", range(1, lax.axis_size("fsdp")))


def sum_tp(vector):
    return sum_direct(
        sum_direct(vector, "tp", (1,)), "tp", range(2, lax.axis_size("tp"), 2)
    )


def block_table(seq_len, seq_group, group_id, block_count):
    seq_order = jnp.arange(seq_len.shape[0], dtype=jnp.int32)
    same_before = (seq_group[None, :] == seq_group[:, None]) & (
        seq_order[None, :] < seq_order[:, None]
    )
    starts = jnp.sum(jnp.where(same_before, seq_len[None, :], 0), axis=1) // BLOCK
    ends = starts + seq_len // BLOCK
    block_at = jnp.arange(block_count, dtype=jnp.int32)
    inside = (
        (seq_group[None, :] == group_id)
        & (starts[None, :] <= block_at[:, None])
        & (block_at[:, None] < ends[None, :])
    )
    held = jnp.sum(inside.astype(jnp.int32), axis=1)
    first = jnp.sum(jnp.where(inside, starts[None, :], 0), axis=1)
    first = jnp.where(held > 0, first, block_at)
    place = block_at
    if lax.axis_size("tp") == SWAP_TP:
        apart = block_at ^ lax.axis_index("tp")
        place = (apart >> 1) + 4 * (apart & 1)
    return jnp.stack([place, first, held]).astype(jnp.int32)


def dot_nt(left, right):
    return lax.dot_general(
        left, right, (((1,), (1,)), ((), ())), preferred_element_type=jnp.float32
    )


def block_rows(place):
    return pl.ds(pl.multiple_of(place * BLOCK, BLOCK), BLOCK)


def attend_kernel(table, qkv, ctx, lse):
    head_cols = ctx.shape[1]
    heads = head_cols // HEAD_DIM
    sharpness = HEAD_DIM ** (-0.5) * LOG2_E
    key_row = lax.broadcasted_iota(jnp.int32, (BLOCK, BLOCK), 0)
    query_col = lax.broadcasted_iota(jnp.int32, (BLOCK, BLOCK), 1)

    def cols(part, head):
        return pl.ds(part * head_cols + head * HEAD_DIM, HEAD_DIM)

    def query_block(at, _):
        rows = block_rows(table[0, at])
        queries = [qkv[rows, cols(0, head)] for head in range(heads)]
        allowed = (key_row == query_col) | ((key_row < query_col) & (table[2, at] > 0))

        def start(head):
            scores = dot_nt(qkv[rows, cols(1, head)], queries[head]) * sharpness
            scores = jnp.where(allowed, scores, MASKED)
            top = jnp.max(scores, axis=0, keepdims=True)
            weights = jnp.exp2(scores - top)
            total = jnp.sum(weights, axis=0, keepdims=True)
            return top, total, contract_rows(qkv[rows, cols(2, head)], weights.astype(jnp.bfloat16))

        def key_block(key_at, carried):
            key_rows = block_rows(table[0, key_at])
            result = []
            for head in range(heads):
                top, total, mixed = carried[head]
                scores = dot_nt(qkv[key_rows, cols(1, head)], queries[head]) * sharpness
                new_top = jnp.maximum(top, jnp.max(scores, axis=0, keepdims=True))
                shrink = jnp.exp2(top - new_top)
                weights = jnp.exp2(scores - new_top)
                total = total * shrink + jnp.sum(weights, axis=0, keepdims=True)
                mixed = mixed * shrink + contract_rows(
                    qkv[key_rows, cols(2, head)], weights.astype(jnp.bfloat16)
                )
                result.append((new_top, total, mixed))
            return tuple(result)

        done = lax.fori_loop(
            table[1, at], at, key_block, tuple(start(head) for head in range(heads))
        )
        for head in range(heads):
            top, total, mixed = done[head]
            ctx[rows, pl.ds(head * HEAD_DIM, HEAD_DIM)] = (mixed / total).T.astype(jnp.bfloat16)
            lse[pl.ds(head * 8, 8), rows] = jnp.broadcast_to(top + jnp.log2(total), (8, BLOCK))
        return 0

    lax.fori_loop(0, table.shape[1], query_block, 0)


def attend_back_kernel(table, qkv, ctx, ctx_grad, lse, qkv_grad, sums, key_acc, value_acc):
    head_cols = ctx.shape[1]
    heads = head_cols // HEAD_DIM
    scaling = HEAD_DIM ** (-0.5)
    sharpness = scaling * LOG2_E
    key_row = lax.broadcasted_iota(jnp.int32, (BLOCK, BLOCK), 0)
    query_col = lax.broadcasted_iota(jnp.int32, (BLOCK, BLOCK), 1)
    sums[...] = jnp.zeros_like(sums)

    def cols(part, head):
        return pl.ds(part * head_cols + head * HEAD_DIM, HEAD_DIM)

    def query_block(at, _):
        rows = block_rows(table[0, at])
        queries, grads, levels, dots = [], [], [], []
        for head in range(heads):
            own = pl.ds(head * HEAD_DIM, HEAD_DIM)
            queries.append(qkv[rows, cols(0, head)])
            grads.append(ctx_grad[rows, own])
            levels.append(lse[pl.ds(head * 8, 1), rows])
            dot = jnp.sum(
                grads[head].astype(jnp.float32) * ctx[rows, own].astype(jnp.float32),
                axis=-1,
                keepdims=True,
            )
            dots.append(jnp.broadcast_to(dot, (BLOCK, HEAD_DIM)).T[:1])
        allowed = (key_row == query_col) | ((key_row < query_col) & (table[2, at] > 0))

        def tile(head, key_rows, masked):
            keys = qkv[key_rows, cols(1, head)]
            probs = jnp.exp2(dot_nt(keys, queries[head]) * sharpness - levels[head])
            if masked:
                probs = jnp.where(allowed, probs, 0.0)
            prob_grad = dot_nt(qkv[key_rows, cols(2, head)], grads[head])
            score_grad = (probs * (prob_grad - dots[head])).astype(jnp.bfloat16)
            value_part = jnp.dot(
                probs.astype(jnp.bfloat16), grads[head], preferred_element_type=jnp.float32
            )
            key_part = jnp.dot(score_grad, queries[head], preferred_element_type=jnp.float32)
            return contract_rows(score_grad, keys), key_part, value_part

        query_acc = []
        for head in range(heads):
            own = pl.ds(head * HEAD_DIM, HEAD_DIM)
            query_part, key_part, value_part = tile(head, rows, True)
            key_acc[rows, own] = key_part
            value_acc[rows, own] = value_part
            query_acc.append(query_part)

        def key_block(key_at, carried):
            key_rows = block_rows(table[0, key_at])
            result = []
            for head in range(heads):
                own = pl.ds(head * HEAD_DIM, HEAD_DIM)
                query_part, key_part, value_part = tile(head, key_rows, False)
                key_acc[key_rows, own] += key_part
                value_acc[key_rows, own] += value_part
                result.append(carried[head] + query_part)
            return tuple(result)

        query_acc = lax.fori_loop(table[1, at], at, key_block, tuple(query_acc))
        for head in range(heads):
            low = (query_acc[head] * scaling).astype(jnp.bfloat16)
            qkv_grad[rows, cols(0, head)] = low
            sums[:1, pl.ds(head * HEAD_DIM, HEAD_DIM)] += jnp.sum(
                low.astype(jnp.float32), axis=0, keepdims=True
            )
        return 0

    lax.fori_loop(0, table.shape[1], query_block, 0)

    def finish(at, _):
        rows = block_rows(at)
        key_low = (key_acc[rows, :] * scaling).astype(jnp.bfloat16)
        value_low = value_acc[rows, :].astype(jnp.bfloat16)
        qkv_grad[rows, pl.ds(head_cols, head_cols)] = key_low
        qkv_grad[rows, pl.ds(2 * head_cols, head_cols)] = value_low
        sums[1:2, :] += jnp.sum(value_low.astype(jnp.float32), axis=0, keepdims=True)
        return 0

    lax.fori_loop(0, table.shape[1], finish, 0)


def whole_specs(count):
    return [pl.BlockSpec(memory_space=pltpu.VMEM) for _ in range(count)]


def attend(table, qkv_rows, head_cols):
    rows = qkv_rows.shape[0]
    heads = head_cols // HEAD_DIM
    return pl.pallas_call(
        attend_kernel,
        out_shape=(
            jax.ShapeDtypeStruct((rows, head_cols), jnp.bfloat16),
            jax.ShapeDtypeStruct((8 * heads, rows), jnp.float32),
        ),
        in_specs=[pl.BlockSpec(memory_space=pltpu.SMEM), *whole_specs(1)],
        out_specs=tuple(whole_specs(2)),
        name="attend",
    )(table, qkv_rows)


def attend_back(table, qkv_rows, context, ctx_grad, lse):
    rows, head_cols = context.shape
    return pl.pallas_call(
        attend_back_kernel,
        out_shape=(
            jax.ShapeDtypeStruct(qkv_rows.shape, jnp.bfloat16),
            jax.ShapeDtypeStruct((8, head_cols), jnp.float32),
        ),
        in_specs=[pl.BlockSpec(memory_space=pltpu.SMEM), *whole_specs(4)],
        out_specs=tuple(whole_specs(2)),
        scratch_shapes=[
            pltpu.VMEM((rows, head_cols), jnp.float32),
            pltpu.VMEM((rows, head_cols), jnp.float32),
        ],
        name="attend_back",
    )(table, qkv_rows, context, ctx_grad, lse)


def local(
    tokens,
    seq_len,
    seq_group,
    ln1_gain,
    ln1_bias,
    qkv_weight,
    qv_bias,
    out_weight,
    out_bias,
    ln2_gain,
    ln2_bias,
    up_weight,
    up_bias,
    down_weight,
    down_bias,
    out_grad,
):
    width = tokens.shape[1]
    head_cols = qkv_weight.shape[2]
    table = block_table(
        seq_len,
        seq_group,
        lax.axis_index("fsdp"),
        tokens.shape[0] * lax.axis_size("tp") // BLOCK,
    )

    def gather_weights():
        return (
            lax.all_gather(qkv_weight, "fsdp", axis=0, tiled=True),
            lax.all_gather(out_weight, "fsdp", axis=1, tiled=True),
            lax.all_gather(up_weight, "fsdp", axis=0, tiled=True),
            lax.all_gather(down_weight, "fsdp", axis=1, tiled=True),
        )

    def sum_weights(partial_sums, axis):
        return lax.psum_scatter(
            partial_sums, "fsdp", scatter_dimension=axis, tiled=True
        )

    inputs = tokens.astype(jnp.float32)
    norm1 = layer_norm(inputs, ln1_gain, ln1_bias).astype(jnp.bfloat16)
    qkv_full, out_full, up_full, down_full = gather_weights()
    qkv_flat = qkv_full.reshape(width, 3 * head_cols)
    qkv_shift = jnp.concatenate([qv_bias[0], jnp.zeros_like(qv_bias[0]), qv_bias[1]])
    norm1_rows = gather_rows(norm1)
    later_grad, norm1_rows = tie(out_grad, norm1_rows)
    grad_state = gather_first(later_grad)
    qkv_rows = (
        jnp.dot(norm1_rows, qkv_flat, preferred_element_type=jnp.float32) + qkv_shift
    ).astype(jnp.bfloat16)
    grad_state, qkv_rows = tie(grad_state, qkv_rows)
    grad_state = gather_second(grad_state)
    context, lse = attend(table, qkv_rows, head_cols)
    grad_state, context = tie(grad_state, context)

    attn_parts = scatter_multiply(
        context,
        lambda part: jnp.dot(part, out_full, preferred_element_type=jnp.float32).astype(
            jnp.bfloat16
        ),
    )
    attn_rows = scatter_last(scatter_second(scatter_first(attn_parts)))
    middle = inputs + attn_rows + out_bias
    norm2 = layer_norm(middle, ln2_gain, ln2_bias).astype(jnp.bfloat16)
    norm2_state = gather_first(norm2)
    grad_piece, norm2_state = tie(gather_last(grad_state), norm2_state)
    norm_piece = gather_last(gather_second(norm2_state))
    pre = jnp.dot(norm_piece, up_full, preferred_element_type=jnp.float32) + up_bias
    act_value, slope = gelu_pair(pre)
    act_rows, slope = tie(act_value.astype(jnp.bfloat16), slope.astype(jnp.bfloat16))

    down_acc = contract_rows(act_rows, grad_piece).astype(jnp.bfloat16)
    down_full, down_acc = tie(down_full, down_acc)
    act_grad = contract_cols(grad_piece, down_full)
    pre_grad = (act_grad * slope.astype(jnp.float32)).astype(jnp.bfloat16)
    shift_acc = jnp.sum(pre_grad.astype(jnp.float32), axis=0)
    norm2_grad_state = scatter_first(
        scatter_multiply(
            pre_grad, lambda part: contract_cols(part, up_full).astype(jnp.bfloat16)
        )
    )
    up_acc = contract_rows(norm_piece, pre_grad).astype(jnp.bfloat16)
    norm2_grad_state, up_acc = tie(norm2_grad_state, up_acc)
    norm2_grad = scatter_last(scatter_second(norm2_grad_state))
    unused_two, ln2_back = jax.vjp(layer_norm, middle, ln2_gain, ln2_bias)
    middle_ln, grad_g2, grad_b2 = ln2_back(norm2_grad)
    grad_rows = out_grad.astype(jnp.float32)
    middle_grad = grad_rows + middle_ln
    portion_state = gather_first(middle_grad.astype(jnp.bfloat16))
    last_part, act_rows = tie(portion_state[-1], act_rows)
    portion_state = (*portion_state[:-1], last_part)
    mlp_pieces = scatter_pieces(
        scatter_multiply(
            act_rows,
            lambda part: jnp.dot(part, down_full, preferred_element_type=jnp.float32).astype(
                jnp.bfloat16
            ),
        )
    )
    portion_state, mlp_pieces = tie(portion_state, mlp_pieces)
    portion = gather_last(gather_second(portion_state))
    shard_down = sum_weights(down_acc, 1)
    portion, mlp_pieces, shard_down = tie(portion, mlp_pieces, shard_down)
    mlp_state = scatter_send(mlp_pieces)
    ctx_grad = contract_cols(portion, out_full).astype(jnp.bfloat16)
    qkv_grad, qv_sums = attend_back(table, qkv_rows, context, ctx_grad, lse)
    mlp_state, qkv_grad = tie(mlp_state, qkv_grad)
    mlp_state = scatter_second(mlp_state)
    shard_up = sum_weights(up_acc, 0)

    def norm1_multiply(part):
        return contract_cols(part, qkv_flat).astype(jnp.bfloat16)

    norm1_far = scatter_pair(qkv_grad, norm1_multiply, 3, 1)
    norm1_far, qkv_grad, late_portion = tie(norm1_far, qkv_grad, portion)
    split = lax.axis_size("tp") == SWAP_TP
    if split:
        half = norm1_far.shape[0] // 2
        far_sums = exchange(norm1_far[:half], 2), exchange(norm1_far[half:], 4)
    else:
        far_sums = scatter_send((norm1_far,))
    out_acc = contract_rows(context, late_portion).astype(jnp.bfloat16)
    out_acc, qkv_grad = tie(out_acc, qkv_grad)
    shard_out = sum_weights(out_acc, 1)
    grad_qkv_w = contract_rows(norm1_rows, qkv_grad).astype(jnp.bfloat16)
    grad_qkv_w, qkv_grad, shard_up, mlp_state, norm1_state = tie(
        grad_qkv_w, qkv_grad, shard_up, mlp_state, far_sums
    )
    if split:
        x_low, y_high, *kept = scatter_pieces(
            (
                norm1_far,
                scatter_pair(qkv_grad, norm1_multiply, 1, 2),
                scatter_pair(qkv_grad, norm1_multiply, 0, 1),
            )
        )[2:]
        norm1_state = (*norm1_state, exchange(x_low, 2), exchange(y_high, 4), *kept)
    layer_out = (middle + scatter_last(mlp_state) + down_bias).astype(jnp.bfloat16)
    norm1_state, shard_out, layer_out = tie(norm1_state, shard_out, layer_out)
    norm1_grad = scatter_last(scatter_second(norm1_state))
    shard_qkv = sum_weights(grad_qkv_w.reshape(width, 3, head_cols), 0)
    unused_one, ln1_back = jax.vjp(layer_norm, inputs, ln1_gain, ln1_bias)
    input_ln, grad_g1, grad_b1 = ln1_back(norm1_grad)
    tokens_grad = (middle_grad + input_ln).astype(jnp.bfloat16)

    wide_sums = [
        jnp.sum(middle_grad, axis=0),
        grad_g2,
        grad_b2,
        jnp.sum(grad_rows, axis=0),
        grad_g1,
        grad_b1,
    ]
    summed = sum_fsdp(jnp.concatenate([*wide_sums, qv_sums[0], qv_sums[1], shift_acc]))
    wide = sum_tp(summed[: 6 * width]).reshape(6, width)
    own = summed[6 * width :]
    return (
        layer_out,
        tokens_grad,
        wide[4],
        wide[5],
        shard_qkv.astype(jnp.float32),
        own[: 2 * head_cols].reshape(2, head_cols),
        shard_out.astype(jnp.float32),
        wide[0],
        wide[1],
        wide[2],
        shard_up.astype(jnp.float32),
        own[2 * head_cols :],
        shard_down.astype(jnp.float32),
        wide[3],
    )


def solution(mesh):
    placed = (
        P(("fsdp", "tp"), None),
        P(),
        P(),
        P(),
        P(),
        P("fsdp", None, "tp"),
        P(None, "tp"),
        P("tp", "fsdp"),
        P(),
        P(),
        P(),
        P("fsdp", "tp"),
        P("tp"),
        P("tp", "fsdp"),
        P(),
        P(("fsdp", "tp"), None),
    )
    return jax.shard_map(
        local,
        mesh=mesh,
        in_specs=placed,
        out_specs=(
            P(("fsdp", "tp"), None),
            P(("fsdp", "tp"), None),
            P(),
            P(),
            P("fsdp", None, "tp"),
            P(None, "tp"),
            P("tp", "fsdp"),
            P(),
            P(),
            P(),
            P("fsdp", "tp"),
            P("tp"),
            P("tp", "fsdp"),
            P(),
        ),
        check_vma=False,
    )
```

```python
import jax
import jax.numpy as jnp
from jax import lax
from jax.experimental import pallas as pl
from jax.experimental.pallas import tpu as pltpu
from jax.sharding import PartitionSpec as P


HEAD_DIM = 128


EPSILON = 1e-05
MASKED = -1e30


def layer_norm(values, gain_vec, bias_vec):
    row_mean = jnp.mean(values, axis=-1, keepdims=True)
    centred = values - row_mean
    variance = jnp.mean(centred * centred, axis=-1, keepdims=True)
    return centred * lax.rsqrt(variance + EPSILON) * gain_vec + bias_vec


def gelu_pair(values):
    squared = values * values
    bent = jnp.tanh(GELU_RATE * values * (1.0 + GELU_CUBE * squared))
    upper = 0.5 * (1.0 + bent)
    slope = upper + 0.5 * values * (1.0 - bent * bent) * GELU_RATE * (1.0 + 3.0 * GELU_CUBE * squared)
    return values * upper, slope


def contract_rows(left, right):
    return lax.dot_general(
        left, right, (((0,), (0,)), ((), ())), preferred_element_type=jnp.float32
    )


def contract_cols(left, right):
    return lax.dot_general(
        left, right, (((1,), (1,)), ((), ())), preferred_element_type=jnp.float32
    )


SWAP_TP = 8
BLOCK = 256
LOG2_E = 1.4426950408889634
GELU_RATE = 0.7978845608028654
GELU_CUBE = 0.044715


def exchange(piece, mask):
    return lax.ppermute(piece, "tp", [(at, at ^ mask) for at in range(SWAP_TP)])


def tie(*values):
    return lax.optimization_barrier(values)


def gather_first(piece):
    if lax.axis_size("tp") != SWAP_TP:
        return (lax.all_gather(piece, "tp", axis=0, tiled=True),)
    return piece, exchange(piece, 2), exchange(piece, 4), exchange(piece, 1)


def gather_second(state):
    if len(state) == 1:
        return state
    piece, from_x, from_y, own_twin = state
    half = piece.shape[0] // 2
    far_low = exchange(from_x[:half], 4)
    far_high = exchange(from_y[half:], 2)
    return piece, from_x, from_y, far_low, far_high, own_twin, exchange(from_x, 1), exchange(from_y, 1)


def gather_pieces(state):
    if len(state) == 1:
        return state
    far_low, far_high = state[3:5]
    return (*state, exchange(far_low, 1), exchange(far_high, 1))


def gather_last(state):
    return jnp.concatenate(gather_pieces(state), axis=0) if len(state) > 1 else state[0]


def gather_rows(piece):
    return gather_last(gather_second(gather_first(piece)))


def add_low(left, right):
    return (left.astype(jnp.float32) + right.astype(jnp.float32)).astype(jnp.bfloat16)


def scatter_pair(left, multiply, first, count):
    if lax.axis_size("tp") != SWAP_TP:
        return multiply(left)
    rows = left.shape[0] // SWAP_TP
    twin = multiply(left[(4 + first) * rows : (4 + first + count) * rows])
    return add_low(multiply(left[first * rows : (first + count) * rows]), exchange(twin, 1))


def scatter_multiply(left, multiply):
    if lax.axis_size("tp") != SWAP_TP:
        return (scatter_pair(left, multiply, 0, 0),)
    return tuple(scatter_pair(left, multiply, first, count) for first, count in ((3, 1), (1, 2), (0, 1)))


def scatter_pieces(parts):
    if len(parts) == 1:
        return parts
    far, mixed, home = parts
    rows = far.shape[0]
    half = rows // 2
    to_x, to_y = mixed[:rows], mixed[rows:]
    return far[:half], far[half:], to_x[:half], to_y[half:], to_x[half:], to_y[:half], home


def scatter_send(pieces):
    if len(pieces) == 1:
        return (lax.psum_scatter(pieces[0], "tp", scatter_dimension=0, tiled=True),)
    far_low, far_high, x_low, y_high, *kept = pieces
    return (
        exchange(far_low, 2),
        exchange(far_high, 4),
        exchange(x_low, 2),
        exchange(y_high, 4),
        *kept,
    )


def scatter_first(parts):
    return scatter_send(scatter_pieces(parts))


def scatter_second(state):
    if len(state) == 1:
        return state
    far_low, far_high, x_low, y_high, to_x, to_y, home = state
    return (
        x_low,
        exchange(add_low(to_x, far_high), 2),
        exchange(add_low(to_y, far_low), 4),
        y_high,
        home,
    )


def scatter_last(state):
    if len(state) == 1:
        return state[0].astype(jnp.float32)
    x_low, x_high, y_low, y_high, home = (part.astype(jnp.float32) for part in state)
    return (
        home
        + jnp.concatenate([x_low, x_high], axis=0)
        + jnp.concatenate([y_low, y_high], axis=0)
    )


def sum_direct(vector, axis, steps):
    count = lax.axis_size(axis)
    terms = [vector] + [
        lax.ppermute(vector, axis, [(at, at ^ step) for at in range(count)]) for step in steps
    ]
    while len(terms) > 1:
        terms = [terms[at] + terms[at + 1] for at in range(0, len(terms), 2)]
    return terms[0]


def sum_fsdp(vector):
    return sum_direct(vector, "fsdp", range(1, lax.axis_size("fsdp")))


def sum_tp(vector):
    return sum_direct(
        sum_direct(vector, "tp", (1,)), "tp", range(2, lax.axis_size("tp"), 2)
    )


def block_table(seq_len, seq_group, group_id, block_count):
    seq_order = jnp.arange(seq_len.shape[0], dtype=jnp.int32)
    same_before = (seq_group[None, :] == seq_group[:, None]) & (
        seq_order[None, :] < seq_order[:, None]
    )
    starts = jnp.sum(jnp.where(same_before, seq_len[None, :], 0), axis=1) // BLOCK
    ends = starts + seq_len // BLOCK
    block_at = jnp.arange(block_count, dtype=jnp.int32)
    inside = (
        (seq_group[None, :] == group_id)
        & (starts[None, :] <= block_at[:, None])
        & (block_at[:, None] < ends[None, :])
    )
    held = jnp.sum(inside.astype(jnp.int32), axis=1)
    first = jnp.sum(jnp.where(inside, starts[None, :], 0), axis=1)
    first = jnp.where(held > 0, first, block_at)
    place = block_at
    if lax.axis_size("tp") == SWAP_TP:
        apart = block_at ^ lax.axis_index("tp")
        place = (apart >> 1) + 4 * (apart & 1)
    return jnp.stack([place, first, held]).astype(jnp.int32)


def dot_nt(left, right):
    return lax.dot_general(
        left, right, (((1,), (1,)), ((), ())), preferred_element_type=jnp.float32
    )


def block_rows(place):
    return pl.ds(pl.multiple_of(place * BLOCK, BLOCK), BLOCK)


def attend_kernel(table, qkv, ctx, lse):
    head_cols = ctx.shape[1]
    heads = head_cols // HEAD_DIM
    sharpness = HEAD_DIM ** (-0.5) * LOG2_E
    key_row = lax.broadcasted_iota(jnp.int32, (BLOCK, BLOCK), 0)
    query_col = lax.broadcasted_iota(jnp.int32, (BLOCK, BLOCK), 1)

    def cols(part, head):
        return pl.ds(part * head_cols + head * HEAD_DIM, HEAD_DIM)

    def query_block(at, _):
        rows = block_rows(table[0, at])
        queries = [qkv[rows, cols(0, head)] for head in range(heads)]
        allowed = (key_row == query_col) | ((key_row < query_col) & (table[2, at] > 0))

        def start(head):
            scores = dot_nt(qkv[rows, cols(1, head)], queries[head]) * sharpness
            scores = jnp.where(allowed, scores, MASKED)
            top = jnp.max(scores, axis=0, keepdims=True)
            weights = jnp.exp2(scores - top)
            total = jnp.sum(weights, axis=0, keepdims=True)
            return top, total, contract_rows(qkv[rows, cols(2, head)], weights.astype(jnp.bfloat16))

        def key_block(key_at, carried):
            key_rows = block_rows(table[0, key_at])
            result = []
            for head in range(heads):
                top, total, mixed = carried[head]
                scores = dot_nt(qkv[key_rows, cols(1, head)], queries[head]) * sharpness
                new_top = jnp.maximum(top, jnp.max(scores, axis=0, keepdims=True))
                shrink = jnp.exp2(top - new_top)
                weights = jnp.exp2(scores - new_top)
                total = total * shrink + jnp.sum(weights, axis=0, keepdims=True)
                mixed = mixed * shrink + contract_rows(
                    qkv[key_rows, cols(2, head)], weights.astype(jnp.bfloat16)
                )
                result.append((new_top, total, mixed))
            return tuple(result)

        done = lax.fori_loop(
            table[1, at], at, key_block, tuple(start(head) for head in range(heads))
        )
        for head in range(heads):
            top, total, mixed = done[head]
            ctx[rows, pl.ds(head * HEAD_DIM, HEAD_DIM)] = (mixed / total).T.astype(jnp.bfloat16)
            lse[pl.ds(head * 8, 8), rows] = jnp.broadcast_to(top + jnp.log2(total), (8, BLOCK))
        return 0

    lax.fori_loop(0, table.shape[1], query_block, 0)


def attend_back_kernel(table, qkv, ctx, ctx_grad, lse, qkv_grad, sums, key_acc, value_acc):
    head_cols = ctx.shape[1]
    heads = head_cols // HEAD_DIM
    scaling = HEAD_DIM ** (-0.5)
    sharpness = scaling * LOG2_E
    key_row = lax.broadcasted_iota(jnp.int32, (BLOCK, BLOCK), 0)
    query_col = lax.broadcasted_iota(jnp.int32, (BLOCK, BLOCK), 1)
    sums[...] = jnp.zeros_like(sums)

    def cols(part, head):
        return pl.ds(part * head_cols + head * HEAD_DIM, HEAD_DIM)

    def query_block(at, _):
        rows = block_rows(table[0, at])
        queries, grads, levels, dots = [], [], [], []
        for head in range(heads):
            own = pl.ds(head * HEAD_DIM, HEAD_DIM)
            queries.append(qkv[rows, cols(0, head)])
            grads.append(ctx_grad[rows, own])
            levels.append(lse[pl.ds(head * 8, 1), rows])
            dot = jnp.sum(
                grads[head].astype(jnp.float32) * ctx[rows, own].astype(jnp.float32),
                axis=-1,
                keepdims=True,
            )
            dots.append(jnp.broadcast_to(dot, (BLOCK, HEAD_DIM)).T[:1])
        allowed = (key_row == query_col) | ((key_row < query_col) & (table[2, at] > 0))

        def tile(head, key_rows, masked):
            keys = qkv[key_rows, cols(1, head)]
            probs = jnp.exp2(dot_nt(keys, queries[head]) * sharpness - levels[head])
            if masked:
                probs = jnp.where(allowed, probs, 0.0)
            prob_grad = dot_nt(qkv[key_rows, cols(2, head)], grads[head])
            score_grad = (probs * (prob_grad - dots[head])).astype(jnp.bfloat16)
            value_part = jnp.dot(
                probs.astype(jnp.bfloat16), grads[head], preferred_element_type=jnp.float32
            )
            key_part = jnp.dot(score_grad, queries[head], preferred_element_type=jnp.float32)
            return contract_rows(score_grad, keys), key_part, value_part

        query_acc = []
        for head in range(heads):
            own = pl.ds(head * HEAD_DIM, HEAD_DIM)
            query_part, key_part, value_part = tile(head, rows, True)
            key_acc[rows, own] = key_part
            value_acc[rows, own] = value_part
            query_acc.append(query_part)

        def key_block(key_at, carried):
            key_rows = block_rows(table[0, key_at])
            result = []
            for head in range(heads):
                own = pl.ds(head * HEAD_DIM, HEAD_DIM)
                query_part, key_part, value_part = tile(head, key_rows, False)
                key_acc[key_rows, own] += key_part
                value_acc[key_rows, own] += value_part
                result.append(carried[head] + query_part)
            return tuple(result)

        query_acc = lax.fori_loop(table[1, at], at, key_block, tuple(query_acc))
        for head in range(heads):
            low = (query_acc[head] * scaling).astype(jnp.bfloat16)
            qkv_grad[rows, cols(0, head)] = low
            sums[:1, pl.ds(head * HEAD_DIM, HEAD_DIM)] += jnp.sum(
                low.astype(jnp.float32), axis=0, keepdims=True
            )
        return 0

    lax.fori_loop(0, table.shape[1], query_block, 0)

    def finish(at, _):
        rows = block_rows(at)
        key_low = (key_acc[rows, :] * scaling).astype(jnp.bfloat16)
        value_low = value_acc[rows, :].astype(jnp.bfloat16)
        qkv_grad[rows, pl.ds(head_cols, head_cols)] = key_low
        qkv_grad[rows, pl.ds(2 * head_cols, head_cols)] = value_low
        sums[1:2, :] += jnp.sum(value_low.astype(jnp.float32), axis=0, keepdims=True)
        return 0

    lax.fori_loop(0, table.shape[1], finish, 0)


def whole_specs(count):
    return [pl.BlockSpec(memory_space=pltpu.VMEM) for _ in range(count)]


def attend(table, qkv_rows, head_cols):
    rows = qkv_rows.shape[0]
    heads = head_cols // HEAD_DIM
    return pl.pallas_call(
        attend_kernel,
        out_shape=(
            jax.ShapeDtypeStruct((rows, head_cols), jnp.bfloat16),
            jax.ShapeDtypeStruct((8 * heads, rows), jnp.float32),
        ),
        in_specs=[pl.BlockSpec(memory_space=pltpu.SMEM), *whole_specs(1)],
        out_specs=tuple(whole_specs(2)),
        name="attend",
    )(table, qkv_rows)


def attend_back(table, qkv_rows, context, ctx_grad, lse):
    rows, head_cols = context.shape
    return pl.pallas_call(
        attend_back_kernel,
        out_shape=(
            jax.ShapeDtypeStruct(qkv_rows.shape, jnp.bfloat16),
            jax.ShapeDtypeStruct((8, head_cols), jnp.float32),
        ),
        in_specs=[pl.BlockSpec(memory_space=pltpu.SMEM), *whole_specs(4)],
        out_specs=tuple(whole_specs(2)),
        scratch_shapes=[
            pltpu.VMEM((rows, head_cols), jnp.float32),
            pltpu.VMEM((rows, head_cols), jnp.float32),
        ],
        name="attend_back",
    )(table, qkv_rows, context, ctx_grad, lse)


def project_back_kernel(*refs):
    *pieces, context, out_full, ctx_grad, out_acc, context_turned, out_turned = refs
    context_turned[...] = context[...].T
    out_turned[...] = out_full[...].T
    spans, first = [], 0
    for piece in pieces:
        spans.append(pl.ds(first, piece.shape[0]))
        first += piece.shape[0]
    for piece, span in zip(pieces, spans):
        ctx_grad[span, :] = jnp.dot(
            piece[...], out_turned[...], preferred_element_type=jnp.float32
        ).astype(jnp.bfloat16)

    def tile(at, _):
        cols = pl.ds(pl.multiple_of(at * BLOCK, BLOCK), BLOCK)
        total = 0.0
        for piece, span in zip(pieces, spans):
            total = total + jnp.dot(
                context_turned[:, span], piece[:, cols], preferred_element_type=jnp.float32
            )
        out_acc[:, cols] = total.astype(jnp.bfloat16)
        return 0

    lax.fori_loop(0, out_acc.shape[1] // BLOCK, tile, 0)


def project_back(pieces, context, out_full):
    return pl.pallas_call(
        project_back_kernel,
        out_shape=(
            jax.ShapeDtypeStruct(context.shape, jnp.bfloat16),
            jax.ShapeDtypeStruct(out_full.shape, jnp.bfloat16),
        ),
        in_specs=whole_specs(len(pieces) + 2),
        out_specs=tuple(whole_specs(2)),
        scratch_shapes=[
            pltpu.VMEM(context.shape[::-1], jnp.bfloat16),
            pltpu.VMEM(out_full.shape[::-1], jnp.bfloat16),
        ],
        name="project_back",
    )(*pieces, context, out_full)


def layer(
    tokens,
    seq_len,
    seq_group,
    ln1_gain,
    ln1_bias,
    qkv_weight,
    qv_bias,
    out_weight,
    out_bias,
    ln2_gain,
    ln2_bias,
    up_weight,
    up_bias,
    down_weight,
    down_bias,
    out_grad,
):
    width = tokens.shape[1]
    head_cols = qkv_weight.shape[2]
    table = block_table(
        seq_len,
        seq_group,
        lax.axis_index("fsdp"),
        tokens.shape[0] * lax.axis_size("tp") // BLOCK,
    )

    def gather_weights():
        return (
            lax.all_gather(qkv_weight, "fsdp", axis=0, tiled=True),
            lax.all_gather(out_weight, "fsdp", axis=1, tiled=True),
            lax.all_gather(up_weight, "fsdp", axis=0, tiled=True),
            lax.all_gather(down_weight, "fsdp", axis=1, tiled=True),
        )

    def sum_weights(partial_sums, axis):
        return lax.psum_scatter(
            partial_sums, "fsdp", scatter_dimension=axis, tiled=True
        )

    inputs = tokens.astype(jnp.float32)
    norm1 = layer_norm(inputs, ln1_gain, ln1_bias).astype(jnp.bfloat16)
    qkv_full, out_full, up_full, down_full = gather_weights()
    qkv_flat = qkv_full.reshape(width, 3 * head_cols)
    qkv_shift = jnp.concatenate([qv_bias[0], jnp.zeros_like(qv_bias[0]), qv_bias[1]])
    norm1_rows = gather_rows(norm1)
    later_grad, norm1_rows = tie(out_grad, norm1_rows)
    grad_state = gather_first(later_grad)
    qkv_rows = (
        jnp.dot(norm1_rows, qkv_flat, preferred_element_type=jnp.float32) + qkv_shift
    ).astype(jnp.bfloat16)
    grad_state, qkv_rows = tie(grad_state, qkv_rows)
    grad_state = gather_second(grad_state)
    context, lse = attend(table, qkv_rows, head_cols)
    grad_state, context = tie(grad_state, context)

    attn_parts = scatter_multiply(
        context,
        lambda part: jnp.dot(part, out_full, preferred_element_type=jnp.float32).astype(
            jnp.bfloat16
        ),
    )
    attn_rows = scatter_last(scatter_second(scatter_first(attn_parts)))
    middle = inputs + attn_rows + out_bias
    norm2 = layer_norm(middle, ln2_gain, ln2_bias).astype(jnp.bfloat16)
    norm2_state = gather_first(norm2)
    grad_piece, norm2_state = tie(gather_last(grad_state), norm2_state)
    norm_piece = gather_last(gather_second(norm2_state))
    pre = jnp.dot(norm_piece, up_full, preferred_element_type=jnp.float32) + up_bias
    act_value, slope = gelu_pair(pre)
    act_rows, slope = tie(act_value.astype(jnp.bfloat16), slope.astype(jnp.bfloat16))

    down_acc = contract_rows(act_rows, grad_piece).astype(jnp.bfloat16)
    down_full, down_acc = tie(down_full, down_acc)
    act_grad = contract_cols(grad_piece, down_full)
    pre_grad = (act_grad * slope.astype(jnp.float32)).astype(jnp.bfloat16)
    shift_acc = jnp.sum(pre_grad.astype(jnp.float32), axis=0)
    norm2_grad_state = scatter_first(
        scatter_multiply(
            pre_grad, lambda part: contract_cols(part, up_full).astype(jnp.bfloat16)
        )
    )
    up_acc = contract_rows(norm_piece, pre_grad).astype(jnp.bfloat16)
    norm2_grad_state, up_acc = tie(norm2_grad_state, up_acc)
    norm2_grad = scatter_last(scatter_second(norm2_grad_state))
    _, ln2_back = jax.vjp(layer_norm, middle, ln2_gain, ln2_bias)
    middle_ln, grad_g2, grad_b2 = ln2_back(norm2_grad)
    grad_rows = out_grad.astype(jnp.float32)
    middle_grad = grad_rows + middle_ln
    portion_state = gather_first(middle_grad.astype(jnp.bfloat16))
    last_part, act_rows = tie(portion_state[-1], act_rows)
    portion_state = (*portion_state[:-1], last_part)
    mlp_pieces = scatter_pieces(
        scatter_multiply(
            act_rows,
            lambda part: jnp.dot(part, down_full, preferred_element_type=jnp.float32).astype(
                jnp.bfloat16
            ),
        )
    )
    portion_state, mlp_pieces = tie(portion_state, mlp_pieces)
    portion = gather_pieces(gather_second(portion_state))
    shard_down = sum_weights(down_acc, 1)
    portion, mlp_pieces, shard_down = tie(portion, mlp_pieces, shard_down)
    mlp_state = scatter_send(mlp_pieces)
    ctx_grad, out_acc = project_back(portion, context, out_full)
    shard_out = sum_weights(out_acc, 1)
    qkv_grad, qv_sums = attend_back(table, qkv_rows, context, ctx_grad, lse)
    mlp_state, qkv_grad = tie(mlp_state, qkv_grad)
    mlp_state = scatter_second(mlp_state)
    shard_up = sum_weights(up_acc, 0)

    def norm1_multiply(part):
        return contract_cols(part, qkv_flat).astype(jnp.bfloat16)

    split = lax.axis_size("tp") == SWAP_TP
    if split:
        far = scatter_pair(qkv_grad, norm1_multiply, 3, 1)
        far, qkv_grad = tie(far, qkv_grad)
        mixed = scatter_pair(qkv_grad, norm1_multiply, 1, 2)
        mixed, qkv_grad = tie(mixed, qkv_grad)
        *norm1_state, home = scatter_send(scatter_pieces((far, mixed, mixed)))
    else:
        norm1_state = list(scatter_first(scatter_multiply(qkv_grad, norm1_multiply)))
    grad_qkv_w = contract_rows(qkv_grad, norm1_rows).astype(jnp.bfloat16)
    grad_qkv_w, qkv_grad, shard_up = tie(grad_qkv_w, qkv_grad, shard_up)
    norm1_state, qkv_grad, mlp_state = tie(norm1_state, qkv_grad, mlp_state)
    if split:
        norm1_state = (*norm1_state, scatter_pair(qkv_grad, norm1_multiply, 0, 1))
    norm1_state = tuple(norm1_state)
    layer_out = (middle + scatter_last(mlp_state) + down_bias).astype(jnp.bfloat16)
    norm1_state, shard_out = tie(norm1_state, shard_out)
    norm1_grad = scatter_last(scatter_second(norm1_state))
    shard_qkv = sum_weights(grad_qkv_w, 1).reshape(3, head_cols, -1).transpose(2, 0, 1)
    _, ln1_back = jax.vjp(layer_norm, inputs, ln1_gain, ln1_bias)
    input_ln, grad_g1, grad_b1 = ln1_back(norm1_grad)
    tokens_grad = (middle_grad + input_ln).astype(jnp.bfloat16)

    wide_sums = [
        jnp.sum(middle_grad, axis=0),
        grad_g2,
        grad_b2,
        jnp.sum(grad_rows, axis=0),
        grad_g1,
        grad_b1,
    ]
    summed = sum_fsdp(jnp.concatenate([*wide_sums, qv_sums[0], qv_sums[1], shift_acc]))
    wide = sum_tp(summed[: 6 * width]).reshape(6, width)
    own = summed[6 * width :]
    return (
        layer_out,
        tokens_grad,
        wide[4],
        wide[5],
        shard_qkv.astype(jnp.float32),
        own[: 2 * head_cols].reshape(2, head_cols),
        shard_out.astype(jnp.float32),
        wide[0],
        wide[1],
        wide[2],
        shard_up.astype(jnp.float32),
        own[2 * head_cols :],
        shard_down.astype(jnp.float32),
        wide[3],
    )


def solution(mesh):
    placed = (
        P(("fsdp", "tp"), None),
        P(),
        P(),
        P(),
        P(),
        P("fsdp", None, "tp"),
        P(None, "tp"),
        P("tp", "fsdp"),
        P(),
        P(),
        P(),
        P("fsdp", "tp"),
        P("tp"),
        P("tp", "fsdp"),
        P(),
        P(("fsdp", "tp"), None),
    )
    return jax.shard_map(
        layer,
        mesh=mesh,
        in_specs=placed,
        out_specs=(
            P(("fsdp", "tp"), None),
            P(("fsdp", "tp"), None),
            P(),
            P(),
            P("fsdp", None, "tp"),
            P(None, "tp"),
            P("tp", "fsdp"),
            P(),
            P(),
            P(),
            P("fsdp", "tp"),
            P("tp"),
            P("tp", "fsdp"),
            P(),
        ),
        check_vma=False,
    )
```

```python
import jax
import jax.numpy as jnp
from jax import lax
from jax.experimental import pallas as pl
from jax.experimental.pallas import tpu as pltpu
from jax.sharding import PartitionSpec as P


HEAD_DIM = 128


EPSILON = 1e-05
MASKED = -1e30


def layer_norm(values, gain_vec, bias_vec):
    row_mean = jnp.mean(values, axis=-1, keepdims=True)
    centred = values - row_mean
    variance = jnp.mean(centred * centred, axis=-1, keepdims=True)
    return centred * lax.rsqrt(variance + EPSILON) * gain_vec + bias_vec


def gelu_pair(values):
    squared = values * values
    bent = jnp.tanh(GELU_RATE * values * (1.0 + GELU_CUBE * squared))
    upper = 0.5 * (1.0 + bent)
    slope = upper + 0.5 * values * (1.0 - bent * bent) * GELU_RATE * (1.0 + 3.0 * GELU_CUBE * squared)
    return values * upper, slope


def contract_rows(left, right):
    return lax.dot_general(
        left, right, (((0,), (0,)), ((), ())), preferred_element_type=jnp.float32
    )


def contract_cols(left, right):
    return lax.dot_general(
        left, right, (((1,), (1,)), ((), ())), preferred_element_type=jnp.float32
    )


SWAP_TP = 8
BLOCK = 256
LOG2_E = 1.4426950408889634
GELU_RATE = 0.7978845608028654
GELU_CUBE = 0.044715


def exchange(piece, mask):
    return lax.ppermute(piece, "tp", [(at, at ^ mask) for at in range(SWAP_TP)])


def tie(*values):
    return lax.optimization_barrier(values)


def gather_first(piece):
    if lax.axis_size("tp") != SWAP_TP:
        return (lax.all_gather(piece, "tp", axis=0, tiled=True),)
    return piece, exchange(piece, 2), exchange(piece, 4), exchange(piece, 1)


def gather_second(state):
    if len(state) == 1:
        return state
    piece, from_x, from_y, own_twin = state
    half = piece.shape[0] // 2
    far_low = exchange(from_x[:half], 4)
    far_high = exchange(from_y[half:], 2)
    return piece, from_x, from_y, far_low, far_high, own_twin, exchange(from_x, 1), exchange(from_y, 1)


def gather_pieces(state):
    if len(state) == 1:
        return state
    far_low, far_high = state[3:5]
    return (*state, exchange(far_low, 1), exchange(far_high, 1))


def gather_last(state):
    return jnp.concatenate(gather_pieces(state), axis=0) if len(state) > 1 else state[0]


def gather_rows(piece):
    return gather_last(gather_second(gather_first(piece)))


def add_low(left, right):
    return (left.astype(jnp.float32) + right.astype(jnp.float32)).astype(jnp.bfloat16)


def scatter_pair(left, multiply, first, count):
    if lax.axis_size("tp") != SWAP_TP:
        return multiply(left)
    rows = left.shape[0] // SWAP_TP
    twin = multiply(left[(4 + first) * rows : (4 + first + count) * rows])
    return add_low(multiply(left[first * rows : (first + count) * rows]), exchange(twin, 1))


def scatter_multiply(left, multiply):
    if lax.axis_size("tp") != SWAP_TP:
        return (scatter_pair(left, multiply, 0, 0),)
    return tuple(scatter_pair(left, multiply, first, count) for first, count in ((3, 1), (1, 2), (0, 1)))


def scatter_pieces(parts):
    if len(parts) == 1:
        return parts
    far, mixed, home = parts
    rows = far.shape[0]
    half = rows // 2
    to_x, to_y = mixed[:rows], mixed[rows:]
    return far[:half], far[half:], to_x[:half], to_y[half:], to_x[half:], to_y[:half], home


def scatter_send(pieces):
    if len(pieces) == 1:
        return (lax.psum_scatter(pieces[0], "tp", scatter_dimension=0, tiled=True),)
    far_low, far_high, x_low, y_high, *kept = pieces
    return (
        exchange(far_low, 2),
        exchange(far_high, 4),
        exchange(x_low, 2),
        exchange(y_high, 4),
        *kept,
    )


def scatter_first(parts):
    return scatter_send(scatter_pieces(parts))


def scatter_second(state):
    if len(state) == 1:
        return state
    far_low, far_high, x_low, y_high, to_x, to_y, home = state
    return (
        x_low,
        exchange(add_low(to_x, far_high), 2),
        exchange(add_low(to_y, far_low), 4),
        y_high,
        home,
    )


def scatter_last(state):
    if len(state) == 1:
        return state[0].astype(jnp.float32)
    x_low, x_high, y_low, y_high, home = (part.astype(jnp.float32) for part in state)
    return (
        home
        + jnp.concatenate([x_low, x_high], axis=0)
        + jnp.concatenate([y_low, y_high], axis=0)
    )


def scatter_tail(far_sums, left, multiply):
    mixed, left = tie(scatter_pair(left, multiply, 1, 2), left)
    half = mixed.shape[0] // 4
    x_low, x_high, y_low, y_high = (mixed[at * half : (at + 1) * half] for at in range(4))
    low_sums = exchange(x_low, 2), exchange(y_high, 4)
    sums = scatter_second((*far_sums, *low_sums, x_high, y_low, mixed))[:4]
    home = scatter_pair(left, multiply, 0, 1)
    return scatter_last((*sums, home))


def far_sends(left, multiply):
    far, left = tie(scatter_pair(left, multiply, 3, 1), left)
    half = far.shape[0] // 2
    return (exchange(far[:half], 2), exchange(far[half:], 4)), left


def sum_direct(vector, axis, steps):
    count = lax.axis_size(axis)
    terms = [vector] + [
        lax.ppermute(vector, axis, [(at, at ^ step) for at in range(count)]) for step in steps
    ]
    while len(terms) > 1:
        terms = [terms[at] + terms[at + 1] for at in range(0, len(terms), 2)]
    return terms[0]


def sum_fsdp(vector):
    return sum_direct(vector, "fsdp", range(1, lax.axis_size("fsdp")))


def sum_tp(vector):
    return sum_direct(
        sum_direct(vector, "tp", (1,)), "tp", range(2, lax.axis_size("tp"), 2)
    )


def block_table(seq_len, seq_group, group_id, block_count):
    seq_order = jnp.arange(seq_len.shape[0], dtype=jnp.int32)
    same_before = (seq_group[None, :] == seq_group[:, None]) & (
        seq_order[None, :] < seq_order[:, None]
    )
    starts = jnp.sum(jnp.where(same_before, seq_len[None, :], 0), axis=1) // BLOCK
    ends = starts + seq_len // BLOCK
    block_at = jnp.arange(block_count, dtype=jnp.int32)
    inside = (
        (seq_group[None, :] == group_id)
        & (starts[None, :] <= block_at[:, None])
        & (block_at[:, None] < ends[None, :])
    )
    held = jnp.sum(inside.astype(jnp.int32), axis=1)
    first = jnp.sum(jnp.where(inside, starts[None, :], 0), axis=1)
    first = jnp.where(held > 0, first, block_at)
    place = block_at
    if lax.axis_size("tp") == SWAP_TP:
        apart = block_at ^ lax.axis_index("tp")
        place = (apart >> 1) + 4 * (apart & 1)
    return jnp.stack([place, first, held]).astype(jnp.int32)


def dot_nt(left, right):
    return lax.dot_general(
        left, right, (((1,), (1,)), ((), ())), preferred_element_type=jnp.float32
    )


def block_rows(place):
    return pl.ds(pl.multiple_of(place * BLOCK, BLOCK), BLOCK)


def attend_kernel(table, qkv, ctx, lse):
    head_cols = ctx.shape[1]
    heads = head_cols // HEAD_DIM
    sharpness = HEAD_DIM ** (-0.5) * LOG2_E
    key_row = lax.broadcasted_iota(jnp.int32, (BLOCK, BLOCK), 0)
    query_col = lax.broadcasted_iota(jnp.int32, (BLOCK, BLOCK), 1)

    def cols(part, head):
        return pl.ds(part * head_cols + head * HEAD_DIM, HEAD_DIM)

    def query_block(at, _):
        rows = block_rows(table[0, at])
        queries = [qkv[rows, cols(0, head)] for head in range(heads)]
        allowed = (key_row == query_col) | ((key_row < query_col) & (table[2, at] > 0))

        def start(head):
            scores = dot_nt(qkv[rows, cols(1, head)], queries[head]) * sharpness
            scores = jnp.where(allowed, scores, MASKED)
            top = jnp.max(scores, axis=0, keepdims=True)
            weights = jnp.exp2(scores - top)
            total = jnp.sum(weights, axis=0, keepdims=True)
            return top, total, contract_rows(qkv[rows, cols(2, head)], weights.astype(jnp.bfloat16))

        def key_block(key_at, carried):
            key_rows = block_rows(table[0, key_at])
            result = []
            for head in range(heads):
                top, total, mixed = carried[head]
                scores = dot_nt(qkv[key_rows, cols(1, head)], queries[head]) * sharpness
                new_top = jnp.maximum(top, jnp.max(scores, axis=0, keepdims=True))
                shrink = jnp.exp2(top - new_top)
                weights = jnp.exp2(scores - new_top)
                total = total * shrink + jnp.sum(weights, axis=0, keepdims=True)
                mixed = mixed * shrink + contract_rows(
                    qkv[key_rows, cols(2, head)], weights.astype(jnp.bfloat16)
                )
                result.append((new_top, total, mixed))
            return tuple(result)

        done = lax.fori_loop(
            table[1, at], at, key_block, tuple(start(head) for head in range(heads))
        )
        for head in range(heads):
            top, total, mixed = done[head]
            ctx[rows, pl.ds(head * HEAD_DIM, HEAD_DIM)] = (mixed / total).T.astype(jnp.bfloat16)
            lse[pl.ds(head * 8, 8), rows] = jnp.broadcast_to(top + jnp.log2(total), (8, BLOCK))
        return 0

    lax.fori_loop(0, table.shape[1], query_block, 0)


def attend_back_kernel(table, qkv, ctx, ctx_grad, lse, qkv_grad, sums, key_acc, value_acc):
    head_cols = ctx.shape[1]
    heads = head_cols // HEAD_DIM
    scaling = HEAD_DIM ** (-0.5)
    sharpness = scaling * LOG2_E
    key_row = lax.broadcasted_iota(jnp.int32, (BLOCK, BLOCK), 0)
    query_col = lax.broadcasted_iota(jnp.int32, (BLOCK, BLOCK), 1)
    sums[...] = jnp.zeros_like(sums)

    def cols(part, head):
        return pl.ds(part * head_cols + head * HEAD_DIM, HEAD_DIM)

    def query_block(at, _):
        rows = block_rows(table[0, at])
        queries, grads, levels, dots = [], [], [], []
        for head in range(heads):
            own = pl.ds(head * HEAD_DIM, HEAD_DIM)
            queries.append(qkv[rows, cols(0, head)])
            grads.append(ctx_grad[rows, own])
            levels.append(lse[pl.ds(head * 8, 1), rows])
            dot = jnp.sum(
                grads[head].astype(jnp.float32) * ctx[rows, own].astype(jnp.float32),
                axis=-1,
                keepdims=True,
            )
            dots.append(jnp.broadcast_to(dot, (BLOCK, HEAD_DIM)).T[:1])
        allowed = (key_row == query_col) | ((key_row < query_col) & (table[2, at] > 0))

        def tile(head, key_rows, masked):
            keys = qkv[key_rows, cols(1, head)]
            probs = jnp.exp2(dot_nt(keys, queries[head]) * sharpness - levels[head])
            if masked:
                probs = jnp.where(allowed, probs, 0.0)
            prob_grad = dot_nt(qkv[key_rows, cols(2, head)], grads[head])
            score_grad = (probs * (prob_grad - dots[head])).astype(jnp.bfloat16)
            value_part = jnp.dot(
                probs.astype(jnp.bfloat16), grads[head], preferred_element_type=jnp.float32
            )
            key_part = jnp.dot(score_grad, queries[head], preferred_element_type=jnp.float32)
            return contract_rows(score_grad, keys), key_part, value_part

        query_acc = []
        for head in range(heads):
            own = pl.ds(head * HEAD_DIM, HEAD_DIM)
            query_part, key_part, value_part = tile(head, rows, True)
            key_acc[rows, own] = key_part
            value_acc[rows, own] = value_part
            query_acc.append(query_part)

        def key_block(key_at, carried):
            key_rows = block_rows(table[0, key_at])
            result = []
            for head in range(heads):
                own = pl.ds(head * HEAD_DIM, HEAD_DIM)
                query_part, key_part, value_part = tile(head, key_rows, False)
                key_acc[key_rows, own] += key_part
                value_acc[key_rows, own] += value_part
                result.append(carried[head] + query_part)
            return tuple(result)

        query_acc = lax.fori_loop(table[1, at], at, key_block, tuple(query_acc))
        for head in range(heads):
            low = (query_acc[head] * scaling).astype(jnp.bfloat16)
            qkv_grad[rows, cols(0, head)] = low
            sums[:1, pl.ds(head * HEAD_DIM, HEAD_DIM)] += jnp.sum(
                low.astype(jnp.float32), axis=0, keepdims=True
            )
        return 0

    lax.fori_loop(0, table.shape[1], query_block, 0)

    def finish(at, _):
        rows = block_rows(at)
        key_low = (key_acc[rows, :] * scaling).astype(jnp.bfloat16)
        value_low = value_acc[rows, :].astype(jnp.bfloat16)
        qkv_grad[rows, pl.ds(head_cols, head_cols)] = key_low
        qkv_grad[rows, pl.ds(2 * head_cols, head_cols)] = value_low
        sums[1:2, :] += jnp.sum(value_low.astype(jnp.float32), axis=0, keepdims=True)
        return 0

    lax.fori_loop(0, table.shape[1], finish, 0)


def whole_specs(count):
    return [pl.BlockSpec(memory_space=pltpu.VMEM) for _ in range(count)]


def attend(table, qkv_rows, head_cols):
    rows = qkv_rows.shape[0]
    heads = head_cols // HEAD_DIM
    return pl.pallas_call(
        attend_kernel,
        out_shape=(
            jax.ShapeDtypeStruct((rows, head_cols), jnp.bfloat16),
            jax.ShapeDtypeStruct((8 * heads, rows), jnp.float32),
        ),
        in_specs=[pl.BlockSpec(memory_space=pltpu.SMEM), *whole_specs(1)],
        out_specs=tuple(whole_specs(2)),
        name="attend",
    )(table, qkv_rows)


def attend_back(table, qkv_rows, context, ctx_grad, lse):
    rows, head_cols = context.shape
    return pl.pallas_call(
        attend_back_kernel,
        out_shape=(
            jax.ShapeDtypeStruct(qkv_rows.shape, jnp.bfloat16),
            jax.ShapeDtypeStruct((8, head_cols), jnp.float32),
        ),
        in_specs=[pl.BlockSpec(memory_space=pltpu.SMEM), *whole_specs(4)],
        out_specs=tuple(whole_specs(2)),
        scratch_shapes=[
            pltpu.VMEM((rows, head_cols), jnp.float32),
            pltpu.VMEM((rows, head_cols), jnp.float32),
        ],
        name="attend_back",
    )(table, qkv_rows, context, ctx_grad, lse)


def project_back_kernel(*refs):
    *pieces, context, out_full, ctx_grad, out_acc, context_turned, out_turned = refs
    context_turned[...] = context[...].T
    out_turned[...] = out_full[...].T
    spans, first = [], 0
    for piece in pieces:
        spans.append(pl.ds(first, piece.shape[0]))
        first += piece.shape[0]
    for piece, span in zip(pieces, spans):
        ctx_grad[span, :] = jnp.dot(
            piece[...], out_turned[...], preferred_element_type=jnp.float32
        ).astype(jnp.bfloat16)

    def tile(at, _):
        cols = pl.ds(pl.multiple_of(at * BLOCK, BLOCK), BLOCK)
        total = 0.0
        for piece, span in zip(pieces, spans):
            total = total + jnp.dot(
                context_turned[:, span], piece[:, cols], preferred_element_type=jnp.float32
            )
        out_acc[:, cols] = total.astype(jnp.bfloat16)
        return 0

    lax.fori_loop(0, out_acc.shape[1] // BLOCK, tile, 0)


def project_back(pieces, context, out_full):
    return pl.pallas_call(
        project_back_kernel,
        out_shape=(
            jax.ShapeDtypeStruct(context.shape, jnp.bfloat16),
            jax.ShapeDtypeStruct(out_full.shape, jnp.bfloat16),
        ),
        in_specs=whole_specs(len(pieces) + 2),
        out_specs=tuple(whole_specs(2)),
        scratch_shapes=[
            pltpu.VMEM(context.shape[::-1], jnp.bfloat16),
            pltpu.VMEM(out_full.shape[::-1], jnp.bfloat16),
        ],
        name="project_back",
    )(*pieces, context, out_full)


def layer(
    tokens,
    seq_len,
    seq_group,
    ln1_gain,
    ln1_bias,
    qkv_weight,
    qv_bias,
    out_weight,
    out_bias,
    ln2_gain,
    ln2_bias,
    up_weight,
    up_bias,
    down_weight,
    down_bias,
    out_grad,
):
    width = tokens.shape[1]
    head_cols = qkv_weight.shape[2]
    table = block_table(
        seq_len,
        seq_group,
        lax.axis_index("fsdp"),
        tokens.shape[0] * lax.axis_size("tp") // BLOCK,
    )

    def gather_weights():
        return (
            lax.all_gather(qkv_weight, "fsdp", axis=0, tiled=True),
            lax.all_gather(out_weight, "fsdp", axis=1, tiled=True),
            lax.all_gather(up_weight, "fsdp", axis=0, tiled=True),
            lax.all_gather(down_weight, "fsdp", axis=1, tiled=True),
        )

    def sum_weights(partial_sums, axis):
        return lax.psum_scatter(
            partial_sums, "fsdp", scatter_dimension=axis, tiled=True
        )

    inputs = tokens.astype(jnp.float32)
    norm1 = layer_norm(inputs, ln1_gain, ln1_bias).astype(jnp.bfloat16)
    qkv_full, out_full, up_full, down_full = gather_weights()
    qkv_flat = qkv_full.reshape(width, 3 * head_cols)
    qkv_shift = jnp.concatenate([qv_bias[0], jnp.zeros_like(qv_bias[0]), qv_bias[1]])
    norm1_rows = gather_rows(norm1)
    later_grad, norm1_rows = tie(out_grad, norm1_rows)
    grad_state = gather_first(later_grad)
    qkv_rows = (
        jnp.dot(norm1_rows, qkv_flat, preferred_element_type=jnp.float32) + qkv_shift
    ).astype(jnp.bfloat16)
    grad_state, qkv_rows = tie(grad_state, qkv_rows)
    grad_state = gather_second(grad_state)
    context, lse = attend(table, qkv_rows, head_cols)
    grad_state, context = tie(grad_state, context)

    attn_parts = scatter_multiply(
        context,
        lambda part: jnp.dot(part, out_full, preferred_element_type=jnp.float32).astype(
            jnp.bfloat16
        ),
    )
    attn_rows = scatter_last(scatter_second(scatter_first(attn_parts)))
    middle = inputs + attn_rows + out_bias
    norm2 = layer_norm(middle, ln2_gain, ln2_bias).astype(jnp.bfloat16)
    norm2_state = gather_first(norm2)
    grad_piece, norm2_state = tie(gather_last(grad_state), norm2_state)
    norm_piece = gather_last(gather_second(norm2_state))
    pre = jnp.dot(norm_piece, up_full, preferred_element_type=jnp.float32) + up_bias
    act_value, slope = gelu_pair(pre)
    act_rows, slope = tie(act_value.astype(jnp.bfloat16), slope.astype(jnp.bfloat16))

    down_acc = contract_rows(act_rows, grad_piece).astype(jnp.bfloat16)
    down_full, down_acc = tie(down_full, down_acc)
    act_grad = contract_cols(grad_piece, down_full)
    pre_grad = (act_grad * slope.astype(jnp.float32)).astype(jnp.bfloat16)
    shift_acc = jnp.sum(pre_grad.astype(jnp.float32), axis=0)
    split = lax.axis_size("tp") == SWAP_TP

    def norm2_multiply(part):
        return contract_cols(part, up_full).astype(jnp.bfloat16)

    if split:
        far_sums, rest = far_sends(pre_grad, norm2_multiply)
        norm2_grad = scatter_tail(far_sums, rest, norm2_multiply)
    else:
        norm2_grad = scatter_last(scatter_first(scatter_multiply(pre_grad, norm2_multiply)))
    up_acc = contract_rows(norm_piece, pre_grad).astype(jnp.bfloat16)
    up_acc, norm2_grad = tie(up_acc, norm2_grad)
    _, ln2_back = jax.vjp(layer_norm, middle, ln2_gain, ln2_bias)
    middle_ln, grad_g2, grad_b2 = ln2_back(norm2_grad)
    grad_rows = out_grad.astype(jnp.float32)
    middle_grad = grad_rows + middle_ln
    portion_state = gather_first(middle_grad.astype(jnp.bfloat16))
    last_part, act_rows = tie(portion_state[-1], act_rows)
    portion_state = (*portion_state[:-1], last_part)
    mlp_pieces = scatter_pieces(
        scatter_multiply(
            act_rows,
            lambda part: jnp.dot(part, down_full, preferred_element_type=jnp.float32).astype(
                jnp.bfloat16
            ),
        )
    )
    portion_state, mlp_pieces = tie(portion_state, mlp_pieces)
    portion = gather_pieces(gather_second(portion_state))
    shard_down = sum_weights(down_acc, 1)
    portion, mlp_pieces, shard_down = tie(portion, mlp_pieces, shard_down)
    mlp_state = scatter_send(mlp_pieces)
    ctx_grad, out_acc = project_back(portion, context, out_full)
    shard_out = sum_weights(out_acc, 1)
    qkv_grad, qv_sums = attend_back(table, qkv_rows, context, ctx_grad, lse)
    mlp_state, qkv_grad = tie(mlp_state, qkv_grad)
    mlp_state = scatter_second(mlp_state)
    shard_up = sum_weights(up_acc, 0)

    def norm1_multiply(part):
        return contract_cols(part, qkv_flat).astype(jnp.bfloat16)

    if split:
        far_sums, qkv_grad = far_sends(qkv_grad, norm1_multiply)
    grad_qkv_w = contract_rows(qkv_grad, norm1_rows).astype(jnp.bfloat16)
    grad_qkv_w, qkv_grad, shard_up = tie(grad_qkv_w, qkv_grad, shard_up)
    if split:
        norm1_grad = scatter_tail(far_sums, qkv_grad, norm1_multiply)
    else:
        norm1_grad = scatter_last(scatter_first(scatter_multiply(qkv_grad, norm1_multiply)))
    norm1_grad, shard_out, mlp_state = tie(norm1_grad, shard_out, mlp_state)
    layer_out = (middle + scatter_last(mlp_state) + down_bias).astype(jnp.bfloat16)
    shard_qkv = sum_weights(grad_qkv_w, 1).reshape(3, head_cols, -1).transpose(2, 0, 1)
    _, ln1_back = jax.vjp(layer_norm, inputs, ln1_gain, ln1_bias)
    input_ln, grad_g1, grad_b1 = ln1_back(norm1_grad)
    tokens_grad = (middle_grad + input_ln).astype(jnp.bfloat16)

    wide_sums = [
        jnp.sum(middle_grad, axis=0),
        grad_g2,
        grad_b2,
        jnp.sum(grad_rows, axis=0),
        grad_g1,
        grad_b1,
    ]
    summed = sum_fsdp(jnp.concatenate([*wide_sums, qv_sums[0], qv_sums[1], shift_acc]))
    wide = sum_tp(summed[: 6 * width]).reshape(6, width)
    own = summed[6 * width :]
    return (
        layer_out,
        tokens_grad,
        wide[4],
        wide[5],
        shard_qkv.astype(jnp.float32),
        own[: 2 * head_cols].reshape(2, head_cols),
        shard_out.astype(jnp.float32),
        wide[0],
        wide[1],
        wide[2],
        shard_up.astype(jnp.float32),
        own[2 * head_cols :],
        shard_down.astype(jnp.float32),
        wide[3],
    )


def solution(mesh):
    placed = (
        P(("fsdp", "tp"), None),
        P(),
        P(),
        P(),
        P(),
        P("fsdp", None, "tp"),
        P(None, "tp"),
        P("tp", "fsdp"),
        P(),
        P(),
        P(),
        P("fsdp", "tp"),
        P("tp"),
        P("tp", "fsdp"),
        P(),
        P(("fsdp", "tp"), None),
    )
    return jax.shard_map(
        layer,
        mesh=mesh,
        in_specs=placed,
        out_specs=(
            P(("fsdp", "tp"), None),
            P(("fsdp", "tp"), None),
            P(),
            P(),
            P("fsdp", None, "tp"),
            P(None, "tp"),
            P("tp", "fsdp"),
            P(),
            P(),
            P(),
            P("fsdp", "tp"),
            P("tp"),
            P("tp", "fsdp"),
            P(),
        ),
        check_vma=False,
    )
```
